512 devices in a mesh: dp: 32 (over z, y_hi), seq: 16 (over y_lo, x, core).
Axes of the slice: x: 4, y: 4 (y_hi: 2, y_lo: 2; y = y_hi * 2 + y_lo), z: 16, core: 2. Of those that a mesh axis runs over, the one named last changes fastest.
Arguments:
- sequence_in: bfloat16 [32, 8192, 768], P('dp', 'seq'), may hold values from -6 to 6
- output_grad: bfloat16 [32, 8192, 768], P('dp', 'seq'), may hold values from -6 to 6
- skip_mask: int32 [32, 2], P('dp'), may hold values 0 or 1
- in_gain: float32 [2, 768], replicated, may hold values from 0.25 to 1.75
- input_shift_vec: float32 [2, 768], replicated, may hold values from -3 to 3
- mid_gain: float32 [2, 384], replicated, may hold values from 0.25 to 1.75
- mid_offset: float32 [2, 384], replicated, may hold values from -3 to 3
- conv_weight: bfloat16 [2, 3, 768, 384], P(None, None, 'seq'), may hold values from -0.21875 to 0.21875
- point_weight: bfloat16 [384, 2, 768], P('seq'), may hold values from -0.3125 to 0.3125
Outputs:
- point_grad: float32 [384, 2, 768], P('seq')
- input_grad: bfloat16 [32, 8192, 768], P('dp', 'seq')
The draws below stay inside these ranges and needn't reach their ends.
Inputs may be any that keep to these rules, and one draw needn't show every extreme that they name: skip_mask[s, b] = 1 means that sample s passes block b unchanged in this step.
All inputs are finite; a program needn't handle non-finite values.
Results may differ from the reference program's by a relative error of at most 0.009.
Values may be sent and summed in bfloat16 or wider, within the bound.
No kernel may reach another device: no remote copies, remote signals or barrier semaphores. Data moves between devices by JAX's collectives and lax.ppermute only.
A program may use at most 64 MiB of HBM per device.

```python
import math
import jax
import jax.numpy as jnp
from jax import lax

C = 768
H = 384
FIRST_DILATION = 1024
SECOND_DILATION = 2048
SAMPLES = 32
LENGTH = 8192


def touch_ends(array, stream_key, smallest, largest):
    longest = array.shape.index(max(array.shape))
    spots = []
    for shift in (0, 1):
        where = [jax.random.randint(jax.random.fold_in(stream_key, axis), (), 0, length) for axis, length in enumerate(array.shape)]
        where[longest] = (where[longest] + shift) % array.shape[longest]
        spots.append(tuple(where))
    return array.at[spots[0]].set(smallest).at[spots[1]].set(largest)


def level_of(key, dims, shards, least, high):
    loudness, own = 1.0, jax.random.fold_in(key, 6)
    for position, blocks in shards:
        draws = jnp.exp(jax.random.uniform(jax.random.fold_in(own, position), (blocks,), jnp.float32, least / len(shards), high / len(shards)))
        loudness = loudness * jnp.repeat(draws, dims[position] // blocks).reshape([-1 if axis == position else 1 for axis in range(len(dims))])
    return loudness


def noise(stream_key, dims, width, reach, cuts=(), held_as=jnp.bfloat16):
    result = width * jax.random.normal(stream_key, dims, jnp.float32)
    if cuts:
        result = result * level_of(stream_key, dims, cuts, -0.22, 0.18)
    return jnp.clip(result, -reach, reach).astype(held_as)


def setup_inputs(seed: int = 0) -> dict:
    arg_keys = jax.random.split(jax.random.key(seed), 10)
    return {
        "sequence_in": noise(arg_keys[0], (SAMPLES, LENGTH, C), 1.0, 6.0, ((0, 32), (1, 16))),
        "output_grad": noise(arg_keys[1], (SAMPLES, LENGTH, C), 1.0, 6.0, ((0, 32), (1, 16))),
        "skip_mask": touch_ends((jax.random.randint(arg_keys[2], (SAMPLES, 2), 0, 4) < 1).astype(jnp.int32), jax.random.fold_in(arg_keys[2], 1), 0, 1),
        "in_gain": jnp.clip(1.0 + 0.15 * jax.random.normal(arg_keys[3], (2, C), jnp.float32), 0.25, 1.75),
        "input_shift_vec": noise(arg_keys[4], (2, C), 0.5, 3.0, (), jnp.float32),
        "mid_gain": jnp.clip(1.0 + 0.15 * jax.random.normal(arg_keys[5], (2, H), jnp.float32), 0.25, 1.75),
        "mid_offset": noise(arg_keys[6], (2, H), 0.5, 3.0, (), jnp.float32),
        "conv_weight": noise(arg_keys[7], (2, 3, C, H), C ** -0.5, 0.21875, ((2, 16),)),
        "point_weight": noise(arg_keys[8], (H, 2, C), H ** -0.5, 0.3125, ((0, 16),)),
    }


def gelu_tanh(values):
    return jax.nn.gelu(values, approximate=True)

def dilated_taps(source, distance):
    length = source.shape[0]
    if distance >= length:
        return (jnp.zeros_like(source), jnp.zeros_like(source))
    padding = jnp.zeros((distance, source.shape[1]), source.dtype)
    earlier = jnp.concatenate([padding, source[:length - distance]], axis=0)
    later = jnp.concatenate([source[distance:], padding], axis=0)
    return (earlier, later)

def contract_last(left, right):
    return lax.dot_general(left, right, (((1,), (1,)), ((), ())), preferred_element_type=jnp.float32)

def reference(sequence_in, output_grad, skip_mask, in_gain, input_shift_vec, mid_gain, mid_offset, conv_weight, point_weight):
    dilation_list = (FIRST_DILATION, SECOND_DILATION)

    def single_sample(carry, inputs):
        sample_in, sample_grad, sample_skip = inputs
        state = sample_in
        stored = []
        for block_index in range(2):
            kept_flag = (1 - sample_skip[block_index]).astype(jnp.float32)
            normed = state.astype(jnp.float32) * in_gain[block_index] + input_shift_vec[block_index]
            activated = gelu_tanh(normed).astype(jnp.bfloat16)
            earlier, later = dilated_taps(activated, dilation_list[block_index])
            weight = conv_weight[block_index]
            conv_out = jnp.dot(earlier, weight[0], preferred_element_type=jnp.float32)
            conv_out = conv_out + jnp.dot(activated, weight[1], preferred_element_type=jnp.float32)
            conv_out = conv_out + jnp.dot(later, weight[2], preferred_element_type=jnp.float32)
            middle = conv_out * mid_gain[block_index] + mid_offset[block_index]
            hidden_act = gelu_tanh(middle).astype(jnp.bfloat16)
            branch = jnp.dot(hidden_act, point_weight[:, block_index, :], preferred_element_type=jnp.float32)
            stored.append((normed, middle, hidden_act, kept_flag))
            state = (state.astype(jnp.float32) + kept_flag * branch).astype(jnp.bfloat16)
        gradient = sample_grad
        terms = [None, None]
        for block_index in (1, 0):
            normed, middle, hidden_act, kept_flag = stored[block_index]
            branch_grad = (kept_flag * gradient.astype(jnp.float32)).astype(jnp.bfloat16)
            terms[block_index] = lax.dot_general(hidden_act, branch_grad, (((0,), (0,)), ((), ())), preferred_element_type=jnp.float32)
            hidden_grad = contract_last(branch_grad, point_weight[:, block_index, :])
            middle_grad = jax.vjp(gelu_tanh, middle)[1](hidden_grad)[0]
            conv_grad = (middle_grad * mid_gain[block_index]).astype(jnp.bfloat16)
            earlier, later = dilated_taps(conv_grad, dilation_list[block_index])
            weight = conv_weight[block_index]
            act_grad = contract_last(later, weight[0]) + contract_last(conv_grad, weight[1]) + contract_last(earlier, weight[2])
            normed_grad = jax.vjp(gelu_tanh, normed)[1](act_grad)[0] * in_gain[block_index]
            gradient = (gradient.astype(jnp.float32) + normed_grad).astype(jnp.bfloat16)
        return (carry + jnp.stack(terms, axis=1), gradient)
    start_sum = jnp.zeros((H, 2, C), jnp.float32)
    summed, input_grad = lax.scan(single_sample, start_sum, (sequence_in, output_grad, skip_mask))
    point_grad = summed * (1.0 / math.sqrt(SAMPLES * LENGTH))
    return (point_grad, input_grad)
```

```python
import math

import jax
import jax.numpy as jnp
from jax import lax
from jax.sharding import PartitionSpec as P

FIRST_DILATION = 1024
SECOND_DILATION = 2048


def passed_along(value, axis, by):
    peers = lax.axis_size(axis)
    pairs = [(i, i + by) for i in range(peers) if 0 <= i + by < peers]
    return lax.ppermute(value, axis, pairs)


def gathered(value, axis):
    peers = lax.axis_size(axis)
    copies = jnp.broadcast_to(value[None], (peers,) + value.shape)
    return lax.all_to_all(copies, axis, 0, 0, tiled=True)


def summed_over(value, axis):
    peers = lax.axis_size(axis)
    pieces = value.reshape((peers, -1) + value.shape[1:])
    return lax.all_to_all(pieces, axis, 0, 0, tiled=True).sum(axis=0)


def gelu_tanh(values):
    return jax.nn.gelu(values, approximate=True)


def contract_last(left, right):
    return lax.dot_general(
        left, right, (((1,), (1,)), ((), ())), preferred_element_type=jnp.float32
    )


def neighbours(source, shards_away):
    earlier = passed_along(source, "seq", shards_away)
    later = passed_along(source, "seq", -shards_away)
    return (earlier, later)


def forward_local(
    state, earlier, activated, later, weight, gain_vec, offset_vec, projection, kept_flag
):
    conv_out = jnp.dot(earlier, weight[0], preferred_element_type=jnp.float32)
    conv_out = conv_out + jnp.dot(activated, weight[1], preferred_element_type=jnp.float32)
    conv_out = conv_out + jnp.dot(later, weight[2], preferred_element_type=jnp.float32)
    middle = conv_out * gain_vec + offset_vec
    hidden_act = gelu_tanh(middle).astype(jnp.bfloat16)
    branch = jnp.dot(hidden_act, projection, preferred_element_type=jnp.float32)
    result = (state.astype(jnp.float32) + kept_flag * branch).astype(jnp.bfloat16)
    return (middle, hidden_act, result)


def backward_first(gradient, middle, projection, gain_vec, kept_flag):
    branch_grad = (kept_flag * gradient.astype(jnp.float32)).astype(jnp.bfloat16)
    hidden_grad = contract_last(branch_grad, projection)
    middle_grad = jax.vjp(gelu_tanh, middle)[1](hidden_grad)[0]
    conv_grad = (middle_grad * gain_vec).astype(jnp.bfloat16)
    return (conv_grad, branch_grad)


def backward_second(gradient, earlier, conv_grad, later, weight, normed, gain_vec):
    act_grad = (
        contract_last(later, weight[0])
        + contract_last(conv_grad, weight[1])
        + contract_last(earlier, weight[2])
    )
    normed_grad = jax.vjp(gelu_tanh, normed)[1](act_grad)[0] * gain_vec
    return (gradient.astype(jnp.float32) + normed_grad).astype(jnp.bfloat16)


def grad_rows(hidden_act, branch_grad):
    return lax.dot_general(
        hidden_act, branch_grad, (((0,), (0,)), ((), ())), preferred_element_type=jnp.float32
    )


def shards(
    sequence_in,
    output_grad,
    skip_mask,
    in_gain,
    input_shift_vec,
    mid_gain,
    mid_offset,
    conv_weight,
    point_weight,
):
    position_list = sequence_in.shape[1]
    channels = sequence_in.shape[2]
    point_full = gathered(point_weight, "seq").reshape(-1, *point_weight.shape[1:])
    conv_parts = gathered(conv_weight, "seq")
    conv_full = jnp.moveaxis(conv_parts, 0, 2).reshape(
        conv_weight.shape[0], conv_weight.shape[1], -1, conv_weight.shape[3]
    )
    neighbour_reach = (FIRST_DILATION // position_list, SECOND_DILATION // position_list)
    state = sequence_in.reshape(-1, channels)
    total_rows = state.shape[0]
    saved = []
    for block_index in range(2):
        kept_flag = (1 - skip_mask[0, block_index]).astype(jnp.float32)
        normed = state.astype(jnp.float32) * in_gain[block_index] + input_shift_vec[block_index]
        activated = gelu_tanh(normed).astype(jnp.bfloat16)
        earlier, later = neighbours(
            activated.reshape(sequence_in.shape), neighbour_reach[block_index]
        )
        earlier = earlier.reshape(total_rows, channels)
        later = later.reshape(total_rows, channels)
        weight = conv_full[block_index]
        operands = (
            state,
            earlier,
            activated,
            later,
            weight,
            mid_gain[block_index],
            mid_offset[block_index],
            point_full[:, block_index, :],
            kept_flag,
        )
        middle, hidden_act, state = forward_local(*operands)
        saved.append((normed, middle, hidden_act, kept_flag))
    gradient = output_grad.reshape(-1, channels)
    hidden_saved = [None, None]
    branch_saved = [None, None]
    for block_index in (1, 0):
        normed, middle, hidden_act, kept_flag = saved[block_index]
        projection = point_full[:, block_index, :]
        first_operands = (gradient, middle, projection, mid_gain[block_index], kept_flag)
        conv_grad, branch_grad = backward_first(*first_operands)
        hidden_saved[block_index] = hidden_act
        branch_saved[block_index] = branch_grad
        earlier, later = neighbours(
            conv_grad.reshape(sequence_in.shape[0], position_list, -1), neighbour_reach[block_index]
        )
        earlier = earlier.reshape(total_rows, -1)
        later = later.reshape(total_rows, -1)
        weight = conv_full[block_index]
        second_operands = (
            gradient,
            earlier,
            conv_grad,
            later,
            weight,
            normed,
            in_gain[block_index],
        )
        gradient = backward_second(*second_operands)
    first_term = grad_rows(hidden_saved[0], branch_saved[0])
    second_term = grad_rows(hidden_saved[1], branch_saved[1])
    shared_part = summed_over(jnp.stack([first_term, second_term], axis=1), "seq")
    dp_size = lax.axis_size("dp")
    own_piece = summed_over(shared_part.reshape(dp_size, -1), "dp")
    summed = gathered(own_piece, "dp").reshape(shared_part.shape)
    sample_count = sequence_in.shape[0] * lax.axis_size("dp")
    full_length = position_list * lax.axis_size("seq")
    point_grad = summed * (1.0 / math.sqrt(sample_count * full_length))
    return (point_grad, gradient.reshape(sequence_in.shape))


def solution(mesh):
    return jax.shard_map(
        shards,
        mesh=mesh,
        in_specs=(
            P("dp", "seq", None),
            P("dp", "seq", None),
            P("dp", None),
            P(),
            P(),
            P(),
            P(),
            P(None, None, "seq", None),
            P("seq", None, None),
        ),
        out_specs=(P("seq", None, None), P("dp", "seq", None)),
        check_vma=False,
    )
```

```python
import math

import jax
import jax.numpy as jnp
from jax import lax
from jax.sharding import PartitionSpec as P

FIRST_DILATION = 1024
SECOND_DILATION = 2048


def passed_along(value, axis, by):
    peers = lax.axis_size(axis)
    pairs = [(i, i + by) for i in range(peers) if 0 <= i + by < peers]
    return lax.ppermute(value, axis, pairs)


def gathered(value, axis):
    peers = lax.axis_size(axis)
    copies = jnp.broadcast_to(value[None], (peers,) + value.shape)
    return lax.all_to_all(copies, axis, 0, 0, tiled=True)


def summed_over(value, axis, sent_as=jnp.float32):
    peers = lax.axis_size(axis)
    pieces = value.reshape((peers, -1) + value.shape[1:]).astype(sent_as)
    arrived = lax.all_to_all(pieces, axis, 0, 0, tiled=True)
    return arrived.astype(jnp.float32).sum(axis=0)


def reduced_term(term):
    shared_part = summed_over(term, "seq", jnp.bfloat16)
    dp_size = lax.axis_size("dp")
    own_piece = summed_over(shared_part.reshape(dp_size, -1), "dp")
    return gathered(own_piece, "dp").reshape(shared_part.shape)


def gelu_tanh(values):
    return jax.nn.gelu(values, approximate=True)


def contract_last(left, right):
    return lax.dot_general(
        left, right, (((1,), (1,)), ((), ())), preferred_element_type=jnp.float32
    )


def neighbours(source, shards_away):
    earlier = passed_along(source, "seq", shards_away)
    later = passed_along(source, "seq", -shards_away)
    return (earlier, later)


def forward_local(
    state, earlier, activated, later, weight, gain_vec, offset_vec, projection, kept_flag
):
    conv_out = jnp.dot(earlier, weight[0], preferred_element_type=jnp.float32)
    conv_out = conv_out + jnp.dot(activated, weight[1], preferred_element_type=jnp.float32)
    conv_out = conv_out + jnp.dot(later, weight[2], preferred_element_type=jnp.float32)
    middle = conv_out * gain_vec + offset_vec
    hidden_act = gelu_tanh(middle).astype(jnp.bfloat16)
    branch = jnp.dot(hidden_act, projection, preferred_element_type=jnp.float32)
    result = (state.astype(jnp.float32) + kept_flag * branch).astype(jnp.bfloat16)
    return (middle, hidden_act, result)


def backward_first(gradient, middle, projection, gain_vec, kept_flag):
    branch_grad = (kept_flag * gradient.astype(jnp.float32)).astype(jnp.bfloat16)
    hidden_grad = contract_last(branch_grad, projection)
    middle_grad = jax.vjp(gelu_tanh, middle)[1](hidden_grad)[0]
    conv_grad = (middle_grad * gain_vec).astype(jnp.bfloat16)
    return (conv_grad, branch_grad)


def backward_second(gradient, earlier, conv_grad, later, weight, normed, gain_vec):
    act_grad = (
        contract_last(later, weight[0])
        + contract_last(conv_grad, weight[1])
        + contract_last(earlier, weight[2])
    )
    normed_grad = jax.vjp(gelu_tanh, normed)[1](act_grad)[0] * gain_vec
    return (gradient.astype(jnp.float32) + normed_grad).astype(jnp.bfloat16)


def grad_rows(hidden_act, branch_grad):
    return lax.dot_general(
        hidden_act, branch_grad, (((0,), (0,)), ((), ())), preferred_element_type=jnp.float32
    )


def shards(
    sequence_in,
    output_grad,
    skip_mask,
    in_gain,
    input_shift_vec,
    mid_gain,
    mid_offset,
    conv_weight,
    point_weight,
):
    position_list = sequence_in.shape[1]
    channels = sequence_in.shape[2]
    def conv_gathered(shard):
        return jnp.moveaxis(gathered(shard, "seq"), 0, 1).reshape(
            conv_weight.shape[1], -1, conv_weight.shape[3]
        )

    first_conv = conv_gathered(conv_weight[0])
    point_shard, first_conv = lax.optimization_barrier((point_weight, first_conv))
    point_full = gathered(point_shard, "seq").reshape(-1, *point_weight.shape[1:])
    second_shard, point_full = lax.optimization_barrier((conv_weight[1], point_full))
    conv_full = [first_conv, conv_gathered(second_shard)]
    neighbour_reach = (FIRST_DILATION // position_list, SECOND_DILATION // position_list)
    state = sequence_in.reshape(-1, channels)
    total_rows = state.shape[0]
    saved = []
    for block_index in range(2):
        kept_flag = (1 - skip_mask[0, block_index]).astype(jnp.float32)
        normed = state.astype(jnp.float32) * in_gain[block_index] + input_shift_vec[block_index]
        activated = gelu_tanh(normed).astype(jnp.bfloat16)
        earlier, later = neighbours(
            activated.reshape(sequence_in.shape), neighbour_reach[block_index]
        )
        earlier = earlier.reshape(total_rows, channels)
        later = later.reshape(total_rows, channels)
        weight = conv_full[block_index]
        operands = (
            state,
            earlier,
            activated,
            later,
            weight,
            mid_gain[block_index],
            mid_offset[block_index],
            point_full[:, block_index, :],
            kept_flag,
        )
        middle, hidden_act, state = forward_local(*operands)
        saved.append((normed, middle, hidden_act, kept_flag))
    gradient = output_grad.reshape(-1, channels)
    reduced_terms = [None, None]
    for block_index in (1, 0):
        normed, middle, hidden_act, kept_flag = saved[block_index]
        projection = point_full[:, block_index, :]
        first_operands = (gradient, middle, projection, mid_gain[block_index], kept_flag)
        conv_grad, branch_grad = backward_first(*first_operands)
        reduced_terms[block_index] = reduced_term(grad_rows(hidden_act, branch_grad))
        earlier, later = neighbours(
            conv_grad.reshape(sequence_in.shape[0], position_list, -1), neighbour_reach[block_index]
        )
        earlier = earlier.reshape(total_rows, -1)
        later = later.reshape(total_rows, -1)
        weight = conv_full[block_index]
        second_operands = (
            gradient,
            earlier,
            conv_grad,
            later,
            weight,
            normed,
            in_gain[block_index],
        )
        gradient = backward_second(*second_operands)
    summed = jnp.stack([reduced_terms[0], reduced_terms[1]], axis=1)
    sample_count = sequence_in.shape[0] * lax.axis_size("dp")
    full_length = position_list * lax.axis_size("seq")
    point_grad = summed * (1.0 / math.sqrt(sample_count * full_length))
    return (point_grad, gradient.reshape(sequence_in.shape))


def solution(mesh):
    return jax.shard_map(
        shards,
        mesh=mesh,
        in_specs=(
            P("dp", "seq", None),
            P("dp", "seq", None),
            P("dp", None),
            P(),
            P(),
            P(),
            P(),
            P(None, None, "seq", None),
            P("seq", None, None),
        ),
        out_specs=(P("seq", None, None), P("dp", "seq", None)),
        check_vma=False,
    )
```

```python
import math

import jax
import jax.numpy as jnp
from jax import lax
from jax.sharding import PartitionSpec as P

FIRST_DILATION = 1024
SECOND_DILATION = 2048


def passed_along(value, axis, by):
    peers = lax.axis_size(axis)
    pairs = [(i, i + by) for i in range(peers) if 0 <= i + by < peers]
    return lax.ppermute(value, axis, pairs)


def gathered(value, axis):
    peers = lax.axis_size(axis)
    copies = jnp.broadcast_to(value[None], (peers,) + value.shape)
    return lax.all_to_all(copies, axis, 0, 0, tiled=True)


def summed_over(value, axis, sent_as=jnp.float32):
    peers = lax.axis_size(axis)
    pieces = value.reshape((peers, -1) + value.shape[1:]).astype(sent_as)
    arrived = lax.all_to_all(pieces, axis, 0, 0, tiled=True)
    return arrived.astype(jnp.float32).sum(axis=0)


def reduced_over_dp(value):
    dp_size = lax.axis_size("dp")
    own_piece = summed_over(value.reshape(dp_size, -1), "dp")
    return gathered(own_piece, "dp").reshape(value.shape)


def gelu_tanh(values):
    return jax.nn.gelu(values, approximate=True)


def contract_last(left, right):
    return lax.dot_general(
        left, right, (((1,), (1,)), ((), ())), preferred_element_type=jnp.float32
    )


def neighbours(source, shards_away):
    earlier = passed_along(source, "seq", shards_away)
    later = passed_along(source, "seq", -shards_away)
    return (earlier, later)


def forward_local(
    state, earlier, activated, later, weight, gain_vec, offset_vec, projection, kept_flag
):
    conv_out = jnp.dot(earlier, weight[0], preferred_element_type=jnp.float32)
    conv_out = conv_out + jnp.dot(activated, weight[1], preferred_element_type=jnp.float32)
    conv_out = conv_out + jnp.dot(later, weight[2], preferred_element_type=jnp.float32)
    middle = conv_out * gain_vec + offset_vec
    hidden_act = gelu_tanh(middle).astype(jnp.bfloat16)
    branch = jnp.dot(hidden_act, projection, preferred_element_type=jnp.float32)
    result = (state.astype(jnp.float32) + kept_flag * branch).astype(jnp.bfloat16)
    return (middle, hidden_act, result)


def backward_first(gradient, middle, projection, gain_vec, kept_flag):
    branch_grad = (kept_flag * gradient.astype(jnp.float32)).astype(jnp.bfloat16)
    hidden_grad = contract_last(branch_grad, projection)
    middle_grad = jax.vjp(gelu_tanh, middle)[1](hidden_grad)[0]
    conv_grad = (middle_grad * gain_vec).astype(jnp.bfloat16)
    return (conv_grad, branch_grad)


def backward_second(gradient, earlier, conv_grad, later, weight, normed, gain_vec):
    act_grad = (
        contract_last(later, weight[0])
        + contract_last(conv_grad, weight[1])
        + contract_last(earlier, weight[2])
    )
    normed_grad = jax.vjp(gelu_tanh, normed)[1](act_grad)[0] * gain_vec
    return (gradient.astype(jnp.float32) + normed_grad).astype(jnp.bfloat16)


def grad_rows(hidden_act, branch_grad):
    return lax.dot_general(
        hidden_act, branch_grad, (((0,), (0,)), ((), ())), preferred_element_type=jnp.float32
    )


def shards(
    sequence_in,
    output_grad,
    skip_mask,
    in_gain,
    input_shift_vec,
    mid_gain,
    mid_offset,
    conv_weight,
    point_weight,
):
    position_list = sequence_in.shape[1]
    channels = sequence_in.shape[2]
    def conv_gathered(shard):
        return jnp.moveaxis(gathered(shard, "seq"), 0, 1).reshape(
            conv_weight.shape[1], -1, conv_weight.shape[3]
        )

    conv_size = conv_weight[0].size
    joined = jnp.concatenate([conv_weight[0].reshape(-1), point_weight.reshape(-1)])
    joined_full = gathered(joined, "seq")
    first_conv = jnp.moveaxis(
        joined_full[:, :conv_size].reshape((-1,) + conv_weight.shape[1:]), 0, 1
    ).reshape(conv_weight.shape[1], -1, conv_weight.shape[3])
    point_full = joined_full[:, conv_size:].reshape(-1, *point_weight.shape[1:])
    second_shard, first_conv = lax.optimization_barrier((conv_weight[1], first_conv))
    conv_full = [first_conv, conv_gathered(second_shard)]
    neighbour_reach = (FIRST_DILATION // position_list, SECOND_DILATION // position_list)
    state = sequence_in.reshape(-1, channels)
    total_rows = state.shape[0]
    saved = []
    for block_index in range(2):
        kept_flag = (1 - skip_mask[0, block_index]).astype(jnp.float32)
        normed = state.astype(jnp.float32) * in_gain[block_index] + input_shift_vec[block_index]
        activated = gelu_tanh(normed).astype(jnp.bfloat16)
        earlier, later = neighbours(
            activated.reshape(sequence_in.shape), neighbour_reach[block_index]
        )
        earlier = earlier.reshape(total_rows, channels)
        later = later.reshape(total_rows, channels)
        weight = conv_full[block_index]
        operands = (
            state,
            earlier,
            activated,
            later,
            weight,
            mid_gain[block_index],
            mid_offset[block_index],
            point_full[:, block_index, :],
            kept_flag,
        )
        middle, hidden_act, state = forward_local(*operands)
        saved.append((normed, middle, hidden_act, kept_flag))
    gradient = output_grad.reshape(-1, channels)
    reduced_terms = [None, None]
    for block_index in (1, 0):
        normed, middle, hidden_act, kept_flag = saved[block_index]
        projection = point_full[:, block_index, :]
        first_operands = (gradient, middle, projection, mid_gain[block_index], kept_flag)
        conv_grad, branch_grad = backward_first(*first_operands)
        reduced_terms[block_index] = summed_over(
            grad_rows(hidden_act, branch_grad), "seq", jnp.bfloat16
        )
        earlier, later = neighbours(
            conv_grad.reshape(sequence_in.shape[0], position_list, -1), neighbour_reach[block_index]
        )
        earlier = earlier.reshape(total_rows, -1)
        later = later.reshape(total_rows, -1)
        weight = conv_full[block_index]
        second_operands = (
            gradient,
            earlier,
            conv_grad,
            later,
            weight,
            normed,
            in_gain[block_index],
        )
        gradient = backward_second(*second_operands)
    summed = reduced_over_dp(jnp.stack([reduced_terms[0], reduced_terms[1]], axis=1))
    sample_count = sequence_in.shape[0] * lax.axis_size("dp")
    full_length = position_list * lax.axis_size("seq")
    point_grad = summed * (1.0 / math.sqrt(sample_count * full_length))
    return (point_grad, gradient.reshape(sequence_in.shape))


def solution(mesh):
    return jax.shard_map(
        shards,
        mesh=mesh,
        in_specs=(
            P("dp", "seq", None),
            P("dp", "seq", None),
            P("dp", None),
            P(),
            P(),
            P(),
            P(),
            P(None, None, "seq", None),
            P("seq", None, None),
        ),
        out_specs=(P("seq", None, None), P("dp", "seq", None)),
        check_vma=False,
    )
```

```python
import math

import jax
import jax.numpy as jnp
from jax import lax
from jax.sharding import PartitionSpec as P

FIRST_DILATION = 1024
SECOND_DILATION = 2048


def passed_along(value, axis, by):
    peers = lax.axis_size(axis)
    pairs = [(i, i + by) for i in range(peers) if 0 <= i + by < peers]
    return lax.ppermute(value, axis, pairs)


def gathered(value, axis):
    peers = lax.axis_size(axis)
    copies = jnp.broadcast_to(value[None], (peers,) + value.shape)
    return lax.all_to_all(copies, axis, 0, 0, tiled=True)


def summed_over(value, axis, sent_as=jnp.float32):
    peers = lax.axis_size(axis)
    pieces = value.reshape((peers, -1) + value.shape[1:]).astype(sent_as)
    arrived = lax.all_to_all(pieces, axis, 0, 0, tiled=True)
    return arrived.astype(jnp.float32).sum(axis=0)


def reduced_over_dp(value):
    dp_size = lax.axis_size("dp")
    own_piece = summed_over(value.reshape(dp_size, -1), "dp")
    return gathered(own_piece, "dp").reshape(value.shape)


def gelu_tanh(values):
    return jax.nn.gelu(values, approximate=True)


def contract_last(left, right):
    return lax.dot_general(
        left, right, (((1,), (1,)), ((), ())), preferred_element_type=jnp.float32
    )


def neighbours(source, shards_away):
    earlier = passed_along(source, "seq", shards_away)
    later = passed_along(source, "seq", -shards_away)
    return (earlier, later)


def forward_local(
    state, earlier, activated, later, weight, gain_vec, offset_vec, projection, kept_flag
):
    conv_out = jnp.dot(earlier, weight[0], preferred_element_type=jnp.float32)
    conv_out = conv_out + jnp.dot(activated, weight[1], preferred_element_type=jnp.float32)
    conv_out = conv_out + jnp.dot(later, weight[2], preferred_element_type=jnp.float32)
    middle = conv_out * gain_vec + offset_vec
    hidden_act = gelu_tanh(middle).astype(jnp.bfloat16)
    branch = jnp.dot(hidden_act, projection, preferred_element_type=jnp.float32)
    result = (state.astype(jnp.float32) + kept_flag * branch).astype(jnp.bfloat16)
    return (middle, hidden_act, result)


def backward_first(gradient, middle, projection, gain_vec, kept_flag):
    branch_grad = (kept_flag * gradient.astype(jnp.float32)).astype(jnp.bfloat16)
    hidden_grad = contract_last(branch_grad, projection)
    middle_grad = jax.vjp(gelu_tanh, middle)[1](hidden_grad)[0]
    conv_grad = (middle_grad * gain_vec).astype(jnp.bfloat16)
    return (conv_grad, branch_grad)


def backward_second(gradient, earlier, conv_grad, later, weight, normed, gain_vec):
    act_grad = (
        contract_last(later, weight[0])
        + contract_last(conv_grad, weight[1])
        + contract_last(earlier, weight[2])
    )
    normed_grad = jax.vjp(gelu_tanh, normed)[1](act_grad)[0] * gain_vec
    return (gradient.astype(jnp.float32) + normed_grad).astype(jnp.bfloat16)


def grad_rows(hidden_act, branch_grad):
    return lax.dot_general(
        hidden_act, branch_grad, (((0,), (0,)), ((), ())), preferred_element_type=jnp.float32
    )


def shards(
    sequence_in,
    output_grad,
    skip_mask,
    in_gain,
    input_shift_vec,
    mid_gain,
    mid_offset,
    conv_weight,
    point_weight,
):
    position_list = sequence_in.shape[1]
    channels = sequence_in.shape[2]
    def conv_gathered(shard):
        return jnp.moveaxis(gathered(shard, "seq"), 0, 1).reshape(
            conv_weight.shape[1], -1, conv_weight.shape[3]
        )

    lanes = conv_weight.shape[3]
    conv_rows = conv_weight.shape[1] * conv_weight.shape[2]
    joined = jnp.concatenate(
        [conv_weight[0].reshape(conv_rows, lanes), point_weight.reshape(-1, lanes)]
    )
    joined_full = gathered(joined, "seq")
    first_conv = jnp.moveaxis(
        joined_full[:, :conv_rows].reshape((-1,) + conv_weight.shape[1:]), 0, 1
    ).reshape(conv_weight.shape[1], -1, lanes)
    point_full = joined_full[:, conv_rows:].reshape(-1, *point_weight.shape[1:])
    second_shard, first_conv = lax.optimization_barrier((conv_weight[1], first_conv))
    conv_full = [first_conv, conv_gathered(second_shard)]
    neighbour_reach = (FIRST_DILATION // position_list, SECOND_DILATION // position_list)
    state = sequence_in.reshape(-1, channels)
    total_rows = state.shape[0]
    saved = []
    for block_index in range(2):
        kept_flag = (1 - skip_mask[0, block_index]).astype(jnp.float32)
        normed = state.astype(jnp.float32) * in_gain[block_index] + input_shift_vec[block_index]
        activated = gelu_tanh(normed).astype(jnp.bfloat16)
        earlier, later = neighbours(
            activated.reshape(sequence_in.shape), neighbour_reach[block_index]
        )
        earlier = earlier.reshape(total_rows, channels)
        later = later.reshape(total_rows, channels)
        weight = conv_full[block_index]
        operands = (
            state,
            earlier,
            activated,
            later,
            weight,
            mid_gain[block_index],
            mid_offset[block_index],
            point_full[:, block_index, :],
            kept_flag,
        )
        middle, hidden_act, state = forward_local(*operands)
        saved.append((normed, middle, hidden_act, kept_flag))
    gradient = output_grad.reshape(-1, channels)
    reduced_terms = [None, None]
    for block_index in (1, 0):
        normed, middle, hidden_act, kept_flag = saved[block_index]
        projection = point_full[:, block_index, :]
        first_operands = (gradient, middle, projection, mid_gain[block_index], kept_flag)
        conv_grad, branch_grad = backward_first(*first_operands)
        reduced_terms[block_index] = summed_over(
            grad_rows(hidden_act, branch_grad), "seq", jnp.bfloat16
        )
        earlier, later = neighbours(
            conv_grad.reshape(sequence_in.shape[0], position_list, -1), neighbour_reach[block_index]
        )
        earlier = earlier.reshape(total_rows, -1)
        later = later.reshape(total_rows, -1)
        weight = conv_full[block_index]
        second_operands = (
            gradient,
            earlier,
            conv_grad,
            later,
            weight,
            normed,
            in_gain[block_index],
        )
        gradient = backward_second(*second_operands)
    summed = reduced_over_dp(jnp.stack([reduced_terms[0], reduced_terms[1]], axis=1))
    sample_count = sequence_in.shape[0] * lax.axis_size("dp")
    full_length = position_list * lax.axis_size("seq")
    point_grad = summed * (1.0 / math.sqrt(sample_count * full_length))
    return (point_grad, gradient.reshape(sequence_in.shape))


def solution(mesh):
    return jax.shard_map(
        shards,
        mesh=mesh,
        in_specs=(
            P("dp", "seq", None),
            P("dp", "seq", None),
            P("dp", None),
            P(),
            P(),
            P(),
            P(),
            P(None, None, "seq", None),
            P("seq", None, None),
        ),
        out_specs=(P("seq", None, None), P("dp", "seq", None)),
        check_vma=False,
    )
```

```python
import math

import jax
import jax.numpy as jnp
from jax import lax
from jax.sharding import PartitionSpec as P

FIRST_DILATION = 1024
SECOND_DILATION = 2048


def passed_along(value, axis, by):
    peers = lax.axis_size(axis)
    pairs = [(i, i + by) for i in range(peers) if 0 <= i + by < peers]
    return lax.ppermute(value, axis, pairs)


def gathered(value, axis):
    peers = lax.axis_size(axis)
    copies = jnp.broadcast_to(value[None], (peers,) + value.shape)
    return lax.all_to_all(copies, axis, 0, 0, tiled=True)


def summed_over(value, axis, sent_as=jnp.float32):
    peers = lax.axis_size(axis)
    pieces = value.reshape((peers, -1) + value.shape[1:]).astype(sent_as)
    arrived = lax.all_to_all(pieces, axis, 0, 0, tiled=True)
    return arrived.astype(jnp.float32).sum(axis=0)


def reduced_over_dp(value):
    peers = lax.axis_size("dp")
    distance = 1
    while distance < peers:
        pairs = [(i, i ^ distance) for i in range(peers)]
        value = value + lax.ppermute(value, "dp", pairs)
        distance *= 2
    return value


def gelu_tanh(values):
    return jax.nn.gelu(values, approximate=True)


def contract_last(left, right):
    return lax.dot_general(
        left, right, (((1,), (1,)), ((), ())), preferred_element_type=jnp.float32
    )


def neighbours(source, shards_away):
    earlier = passed_along(source, "seq", shards_away)
    later = passed_along(source, "seq", -shards_away)
    return (earlier, later)


def forward_local(
    state, earlier, activated, later, weight, gain_vec, offset_vec, projection, kept_flag
):
    conv_out = jnp.dot(earlier, weight[0], preferred_element_type=jnp.float32)
    conv_out = conv_out + jnp.dot(activated, weight[1], preferred_element_type=jnp.float32)
    conv_out = conv_out + jnp.dot(later, weight[2], preferred_element_type=jnp.float32)
    middle = conv_out * gain_vec + offset_vec
    hidden_act = gelu_tanh(middle).astype(jnp.bfloat16)
    branch = jnp.dot(hidden_act, projection, preferred_element_type=jnp.float32)
    result = (state.astype(jnp.float32) + kept_flag * branch).astype(jnp.bfloat16)
    return (middle, hidden_act, result)


def backward_first(gradient, middle, projection, gain_vec, kept_flag):
    branch_grad = (kept_flag * gradient.astype(jnp.float32)).astype(jnp.bfloat16)
    hidden_grad = contract_last(branch_grad, projection)
    middle_grad = jax.vjp(gelu_tanh, middle)[1](hidden_grad)[0]
    conv_grad = (middle_grad * gain_vec).astype(jnp.bfloat16)
    return (conv_grad, branch_grad)


def backward_second(gradient, earlier, conv_grad, later, weight, normed, gain_vec):
    act_grad = (
        contract_last(later, weight[0])
        + contract_last(conv_grad, weight[1])
        + contract_last(earlier, weight[2])
    )
    normed_grad = jax.vjp(gelu_tanh, normed)[1](act_grad)[0] * gain_vec
    return (gradient.astype(jnp.float32) + normed_grad).astype(jnp.bfloat16)


def grad_rows(hidden_act, branch_grad):
    return lax.dot_general(
        hidden_act, branch_grad, (((0,), (0,)), ((), ())), preferred_element_type=jnp.float32
    )


def shards(
    sequence_in,
    output_grad,
    skip_mask,
    in_gain,
    input_shift_vec,
    mid_gain,
    mid_offset,
    conv_weight,
    point_weight,
):
    position_list = sequence_in.shape[1]
    channels = sequence_in.shape[2]
    def conv_gathered(shard):
        return jnp.moveaxis(gathered(shard, "seq"), 0, 1).reshape(
            conv_weight.shape[1], -1, conv_weight.shape[3]
        )

    lanes = conv_weight.shape[3]
    conv_rows = conv_weight.shape[1] * conv_weight.shape[2]
    joined = jnp.concatenate(
        [conv_weight[0].reshape(conv_rows, lanes), point_weight.reshape(-1, lanes)]
    )
    joined_full = gathered(joined, "seq")
    first_conv = jnp.moveaxis(
        joined_full[:, :conv_rows].reshape((-1,) + conv_weight.shape[1:]), 0, 1
    ).reshape(conv_weight.shape[1], -1, lanes)
    point_full = joined_full[:, conv_rows:].reshape(-1, *point_weight.shape[1:])
    second_shard, first_conv = lax.optimization_barrier((conv_weight[1], first_conv))
    conv_full = [first_conv, conv_gathered(second_shard)]
    neighbour_reach = (FIRST_DILATION // position_list, SECOND_DILATION // position_list)
    state = sequence_in.reshape(-1, channels)
    total_rows = state.shape[0]
    saved = []
    for block_index in range(2):
        kept_flag = (1 - skip_mask[0, block_index]).astype(jnp.float32)
        normed = state.astype(jnp.float32) * in_gain[block_index] + input_shift_vec[block_index]
        activated = gelu_tanh(normed).astype(jnp.bfloat16)
        earlier, later = neighbours(
            activated.reshape(sequence_in.shape), neighbour_reach[block_index]
        )
        earlier = earlier.reshape(total_rows, channels)
        later = later.reshape(total_rows, channels)
        weight = conv_full[block_index]
        operands = (
            state,
            earlier,
            activated,
            later,
            weight,
            mid_gain[block_index],
            mid_offset[block_index],
            point_full[:, block_index, :],
            kept_flag,
        )
        middle, hidden_act, state = forward_local(*operands)
        saved.append((normed, middle, hidden_act, kept_flag))
    gradient = output_grad.reshape(-1, channels)
    reduced_terms = [None, None]
    for block_index in (1, 0):
        normed, middle, hidden_act, kept_flag = saved[block_index]
        projection = point_full[:, block_index, :]
        first_operands = (gradient, middle, projection, mid_gain[block_index], kept_flag)
        conv_grad, branch_grad = backward_first(*first_operands)
        reduced_terms[block_index] = summed_over(
            grad_rows(hidden_act, branch_grad), "seq", jnp.bfloat16
        )
        earlier, later = neighbours(
            conv_grad.reshape(sequence_in.shape[0], position_list, -1), neighbour_reach[block_index]
        )
        earlier = earlier.reshape(total_rows, -1)
        later = later.reshape(total_rows, -1)
        weight = conv_full[block_index]
        second_operands = (
            gradient,
            earlier,
            conv_grad,
            later,
            weight,
            normed,
            in_gain[block_index],
        )
        gradient = backward_second(*second_operands)
    summed = reduced_over_dp(jnp.stack([reduced_terms[0], reduced_terms[1]], axis=1))
    sample_count = sequence_in.shape[0] * lax.axis_size("dp")
    full_length = position_list * lax.axis_size("seq")
    point_grad = summed * (1.0 / math.sqrt(sample_count * full_length))
    return (point_grad, gradient.reshape(sequence_in.shape))


def solution(mesh):
    return jax.shard_map(
        shards,
        mesh=mesh,
        in_specs=(
            P("dp", "seq", None),
            P("dp", "seq", None),
            P("dp", None),
            P(),
            P(),
            P(),
            P(),
            P(None, None, "seq", None),
            P("seq", None, None),
        ),
        out_specs=(P("seq", None, None), P("dp", "seq", None)),
        check_vma=False,
    )
```

```python
import math

import jax
import jax.numpy as jnp
from jax import lax
from jax.sharding import PartitionSpec as P

FIRST_DILATION = 1024
SECOND_DILATION = 2048


def passed_along(value, axis, by):
    peers = lax.axis_size(axis)
    pairs = [(i, i + by) for i in range(peers) if 0 <= i + by < peers]
    return lax.ppermute(value, axis, pairs)


def gathered(value, axis):
    peers = lax.axis_size(axis)
    copies = jnp.broadcast_to(value[None], (peers,) + value.shape)
    return lax.all_to_all(copies, axis, 0, 0, tiled=True)


def summed_over(value, axis, sent_as=jnp.float32):
    peers = lax.axis_size(axis)
    pieces = value.reshape((peers, -1) + value.shape[1:]).astype(sent_as)
    arrived = lax.all_to_all(pieces, axis, 0, 0, tiled=True)
    return arrived.astype(jnp.float32).sum(axis=0)


def reduced_over_dp(value):
    dp_size = lax.axis_size("dp")
    own_piece = summed_over(value.reshape(dp_size, -1), "dp")
    return gathered(own_piece, "dp").reshape(value.shape)


def gelu_tanh(values):
    return jax.nn.gelu(values, approximate=True)


def contract_last(left, right):
    return lax.dot_general(
        left, right, (((1,), (1,)), ((), ())), preferred_element_type=jnp.float32
    )


def neighbours(source, shards_away):
    earlier = passed_along(source, "seq", shards_away)
    later = passed_along(source, "seq", -shards_away)
    return (earlier, later)


def forward_local(
    state, earlier, activated, later, weight, gain_vec, offset_vec, projection, kept_flag
):
    conv_out = jnp.dot(earlier, weight[0], preferred_element_type=jnp.float32)
    conv_out = conv_out + jnp.dot(activated, weight[1], preferred_element_type=jnp.float32)
    conv_out = conv_out + jnp.dot(later, weight[2], preferred_element_type=jnp.float32)
    middle = conv_out * gain_vec + offset_vec
    hidden_act = gelu_tanh(middle).astype(jnp.bfloat16)
    branch = jnp.dot(hidden_act, projection, preferred_element_type=jnp.float32)
    result = (state.astype(jnp.float32) + kept_flag * branch).astype(jnp.bfloat16)
    return (middle, hidden_act, result)


def backward_first(gradient, middle, projection, gain_vec, kept_flag):
    branch_grad = (kept_flag * gradient.astype(jnp.float32)).astype(jnp.bfloat16)
    hidden_grad = contract_last(branch_grad, projection)
    middle_grad = jax.vjp(gelu_tanh, middle)[1](hidden_grad)[0]
    conv_grad = (middle_grad * gain_vec).astype(jnp.bfloat16)
    return (conv_grad, branch_grad)


def backward_second(gradient, earlier, conv_grad, later, weight, normed, gain_vec):
    act_grad = (
        contract_last(later, weight[0])
        + contract_last(conv_grad, weight[1])
        + contract_last(earlier, weight[2])
    )
    normed_grad = jax.vjp(gelu_tanh, normed)[1](act_grad)[0] * gain_vec
    return (gradient.astype(jnp.float32) + normed_grad).astype(jnp.bfloat16)


def grad_rows(hidden_act, branch_grad):
    return lax.dot_general(
        hidden_act, branch_grad, (((0,), (0,)), ((), ())), preferred_element_type=jnp.float32
    )


def strided(block):
    peers = lax.axis_size("seq")
    channels = block.shape[-1]
    rows = block.reshape(-1, peers, channels).swapaxes(0, 1)
    arrived = lax.all_to_all(rows, "seq", 0, 0, tiled=True)
    return arrived.reshape(-1, channels)


def contiguous(rows):
    peers = lax.axis_size("seq")
    channels = rows.shape[-1]
    pieces = rows.reshape(peers, -1, channels)
    arrived = lax.all_to_all(pieces, "seq", 0, 0, tiled=True)
    return arrived.swapaxes(0, 1).reshape(-1, channels)


def row_shifted(source, rows_away):
    padding = jnp.zeros((rows_away, source.shape[1]), source.dtype)
    earlier = jnp.concatenate([padding, source[: source.shape[0] - rows_away]], axis=0)
    later = jnp.concatenate([source[rows_away:], padding], axis=0)
    return (earlier, later)


def shards(
    sequence_in,
    output_grad,
    skip_mask,
    in_gain,
    input_shift_vec,
    mid_gain,
    mid_offset,
    conv_weight,
    point_weight,
):
    peers = lax.axis_size("seq")
    lanes = conv_weight.shape[3]
    conv_rows = conv_weight.shape[1] * conv_weight.shape[2]
    joined = jnp.concatenate(
        [conv_weight[0].reshape(conv_rows, lanes), point_weight.reshape(-1, lanes)]
    )
    joined_full = gathered(joined, "seq")
    first_conv = jnp.moveaxis(
        joined_full[:, :conv_rows].reshape((-1,) + conv_weight.shape[1:]), 0, 1
    ).reshape(conv_weight.shape[1], -1, lanes)
    point_full = joined_full[:, conv_rows:].reshape(-1, *point_weight.shape[1:])
    second_shard, first_conv = lax.optimization_barrier((conv_weight[1], first_conv))
    conv_full = [first_conv, conv_gathered_block(second_shard, conv_weight.shape)]
    row_reach = (FIRST_DILATION // peers, SECOND_DILATION // peers)
    state = strided(sequence_in[0])
    saved = []
    for block_index in range(2):
        kept_flag = (1 - skip_mask[0, block_index]).astype(jnp.float32)
        normed = state.astype(jnp.float32) * in_gain[block_index] + input_shift_vec[block_index]
        activated = gelu_tanh(normed).astype(jnp.bfloat16)
        earlier, later = row_shifted(activated, row_reach[block_index])
        operands = (
            state,
            earlier,
            activated,
            later,
            conv_full[block_index],
            mid_gain[block_index],
            mid_offset[block_index],
            point_full[:, block_index, :],
            kept_flag,
        )
        middle, hidden_act, state = forward_local(*operands)
        saved.append((normed, middle, hidden_act, kept_flag))
    gradient = strided(output_grad[0])
    reduced_terms = [None, None]
    for block_index in (1, 0):
        normed, middle, hidden_act, kept_flag = saved[block_index]
        projection = point_full[:, block_index, :]
        first_operands = (gradient, middle, projection, mid_gain[block_index], kept_flag)
        conv_grad, branch_grad = backward_first(*first_operands)
        reduced_terms[block_index] = summed_over(
            grad_rows(hidden_act, branch_grad), "seq", jnp.bfloat16
        )
        earlier, later = row_shifted(conv_grad, row_reach[block_index])
        second_operands = (
            gradient,
            earlier,
            conv_grad,
            later,
            conv_full[block_index],
            normed,
            in_gain[block_index],
        )
        gradient = backward_second(*second_operands)
    summed = reduced_over_dp(jnp.stack([reduced_terms[0], reduced_terms[1]], axis=1))
    sample_count = sequence_in.shape[0] * lax.axis_size("dp")
    full_length = sequence_in.shape[1] * peers
    point_grad = summed * (1.0 / math.sqrt(sample_count * full_length))
    return (point_grad, contiguous(gradient).reshape(sequence_in.shape))


def conv_gathered_block(shard, full_shape):
    return jnp.moveaxis(gathered(shard, "seq"), 0, 1).reshape(full_shape[1], -1, full_shape[3])


def solution(mesh):
    return jax.shard_map(
        shards,
        mesh=mesh,
        in_specs=(
            P("dp", "seq", None),
            P("dp", "seq", None),
            P("dp", None),
            P(),
            P(),
            P(),
            P(),
            P(None, None, "seq", None),
            P("seq", None, None),
        ),
        out_specs=(P("seq", None, None), P("dp", "seq", None)),
        check_vma=False,
    )
```

```python
import math

import jax
import jax.numpy as jnp
from jax import lax
from jax.sharding import PartitionSpec as P

FIRST_DILATION = 1024
SECOND_DILATION = 2048


def passed_along(value, axis, by):
    peers = lax.axis_size(axis)
    pairs = [(i, i + by) for i in range(peers) if 0 <= i + by < peers]
    return lax.ppermute(value, axis, pairs)


def gathered(value, axis):
    peers = lax.axis_size(axis)
    copies = jnp.broadcast_to(value[None], (peers,) + value.shape)
    return lax.all_to_all(copies, axis, 0, 0, tiled=True)


def summed_over(value, axis, sent_as=jnp.float32):
    peers = lax.axis_size(axis)
    pieces = value.reshape((peers, -1) + value.shape[1:]).astype(sent_as)
    arrived = lax.all_to_all(pieces, axis, 0, 0, tiled=True)
    return arrived.astype(jnp.float32).sum(axis=0)


def reduced_over_dp(value):
    dp_size = lax.axis_size("dp")
    own_piece = summed_over(value.reshape(dp_size, -1), "dp")
    return gathered(own_piece, "dp").reshape(value.shape)


def gelu_tanh(values):
    return jax.nn.gelu(values, approximate=True)


def contract_last(left, right):
    return lax.dot_general(
        left, right, (((1,), (1,)), ((), ())), preferred_element_type=jnp.float32
    )


def neighbours(source, shards_away):
    earlier = passed_along(source, "seq", shards_away)
    later = passed_along(source, "seq", -shards_away)
    return (earlier, later)


def forward_local(
    state, earlier, activated, later, weight, gain_vec, offset_vec, projection, kept_flag
):
    conv_out = jnp.dot(earlier, weight[0], preferred_element_type=jnp.float32)
    conv_out = conv_out + jnp.dot(activated, weight[1], preferred_element_type=jnp.float32)
    conv_out = conv_out + jnp.dot(later, weight[2], preferred_element_type=jnp.float32)
    middle = conv_out * gain_vec + offset_vec
    hidden_act = gelu_tanh(middle).astype(jnp.bfloat16)
    branch = jnp.dot(hidden_act, projection, preferred_element_type=jnp.float32)
    result = (state.astype(jnp.float32) + kept_flag * branch).astype(jnp.bfloat16)
    return (middle, hidden_act, result)


def backward_first(gradient, middle, projection, gain_vec, kept_flag):
    branch_grad = (kept_flag * gradient.astype(jnp.float32)).astype(jnp.bfloat16)
    hidden_grad = contract_last(branch_grad, projection)
    middle_grad = jax.vjp(gelu_tanh, middle)[1](hidden_grad)[0]
    conv_grad = (middle_grad * gain_vec).astype(jnp.bfloat16)
    return (conv_grad, branch_grad)


def backward_second(gradient, earlier, conv_grad, later, weight, normed, gain_vec):
    act_grad = (
        contract_last(later, weight[0])
        + contract_last(conv_grad, weight[1])
        + contract_last(earlier, weight[2])
    )
    normed_grad = jax.vjp(gelu_tanh, normed)[1](act_grad)[0] * gain_vec
    return (gradient.astype(jnp.float32) + normed_grad).astype(jnp.bfloat16)


def grad_rows(hidden_act, branch_grad):
    return lax.dot_general(
        hidden_act, branch_grad, (((0,), (0,)), ((), ())), preferred_element_type=jnp.float32
    )


def exchanged(parts, axis):
    joined = jnp.concatenate(parts, axis=1)
    arrived = lax.all_to_all(joined, axis, 0, 0, tiled=True)
    pieces = []
    offset = 0
    for part in parts:
        pieces.append(arrived[:, offset : offset + part.shape[1]])
        offset += part.shape[1]
    return pieces


def strided_pieces(block, peers):
    return block.reshape(-1, peers, block.shape[-1]).swapaxes(0, 1)


def same_for_all(shard, peers, lanes):
    flat = shard.reshape(-1, lanes)
    return jnp.broadcast_to(flat[None], (peers,) + flat.shape)


def conv_from_pieces(pieces, block_shape):
    taps, rows, hidden = block_shape
    parts = pieces.reshape(-1, taps, rows, hidden)
    return jnp.moveaxis(parts, 0, 1).reshape(taps, -1, hidden)


def row_shifted(source, rows_away):
    padding = jnp.zeros((rows_away, source.shape[1]), source.dtype)
    earlier = jnp.concatenate([padding, source[: source.shape[0] - rows_away]], axis=0)
    later = jnp.concatenate([source[rows_away:], padding], axis=0)
    return (earlier, later)


def shards(
    sequence_in,
    output_grad,
    skip_mask,
    in_gain,
    input_shift_vec,
    mid_gain,
    mid_offset,
    conv_weight,
    point_weight,
):
    peers = lax.axis_size("seq")
    channels = sequence_in.shape[2]
    block_shape = conv_weight.shape[1:]
    state_pieces, first_pieces, point_pieces = exchanged(
        [
            strided_pieces(sequence_in[0], peers),
            same_for_all(conv_weight[0], peers, channels),
            same_for_all(point_weight, peers, channels),
        ],
        "seq",
    )
    state = state_pieces.reshape(-1, channels)
    point_full = point_pieces.reshape(-1, *point_weight.shape[1:])
    grad_in, second_in, state = lax.optimization_barrier((output_grad[0], conv_weight[1], state))
    grad_pieces, second_pieces = exchanged(
        [strided_pieces(grad_in, peers), same_for_all(second_in, peers, channels)], "seq"
    )
    conv_full = [
        conv_from_pieces(first_pieces, block_shape),
        conv_from_pieces(second_pieces, block_shape),
    ]
    row_reach = (FIRST_DILATION // peers, SECOND_DILATION // peers)
    saved = []
    for block_index in range(2):
        kept_flag = (1 - skip_mask[0, block_index]).astype(jnp.float32)
        normed = state.astype(jnp.float32) * in_gain[block_index] + input_shift_vec[block_index]
        activated = gelu_tanh(normed).astype(jnp.bfloat16)
        earlier, later = row_shifted(activated, row_reach[block_index])
        operands = (
            state,
            earlier,
            activated,
            later,
            conv_full[block_index],
            mid_gain[block_index],
            mid_offset[block_index],
            point_full[:, block_index, :],
            kept_flag,
        )
        middle, hidden_act, state = forward_local(*operands)
        saved.append((normed, middle, hidden_act, kept_flag))
    gradient = grad_pieces.reshape(-1, channels)
    terms = [None, None]
    for block_index in (1, 0):
        normed, middle, hidden_act, kept_flag = saved[block_index]
        projection = point_full[:, block_index, :]
        first_operands = (gradient, middle, projection, mid_gain[block_index], kept_flag)
        conv_grad, branch_grad = backward_first(*first_operands)
        terms[block_index] = grad_rows(hidden_act, branch_grad)
        earlier, later = row_shifted(conv_grad, row_reach[block_index])
        second_operands = (
            gradient,
            earlier,
            conv_grad,
            later,
            conv_full[block_index],
            normed,
            in_gain[block_index],
        )
        gradient = backward_second(*second_operands)
    term_pieces = [
        term.astype(jnp.bfloat16).reshape(peers, -1, channels) for term in terms
    ]
    first_term, second_term, back_pieces = exchanged(
        term_pieces + [gradient.reshape(peers, -1, channels)], "seq"
    )
    own_terms = [
        piece.astype(jnp.float32).sum(axis=0) for piece in (first_term, second_term)
    ]
    summed = reduced_over_dp(jnp.stack(own_terms, axis=1))
    sample_count = sequence_in.shape[0] * lax.axis_size("dp")
    full_length = sequence_in.shape[1] * peers
    point_grad = summed * (1.0 / math.sqrt(sample_count * full_length))
    input_grad = back_pieces.swapaxes(0, 1).reshape(sequence_in.shape)
    return (point_grad, input_grad)


def solution(mesh):
    return jax.shard_map(
        shards,
        mesh=mesh,
        in_specs=(
            P("dp", "seq", None),
            P("dp", "seq", None),
            P("dp", None),
            P(),
            P(),
            P(),
            P(),
            P(None, None, "seq", None),
            P("seq", None, None),
        ),
        out_specs=(P("seq", None, None), P("dp", "seq", None)),
        check_vma=False,
    )
```

```python
import math

import jax
import jax.numpy as jnp
from jax import lax
from jax.sharding import PartitionSpec as P

FIRST_DILATION = 1024
SECOND_DILATION = 2048


def passed_along(value, axis, by):
    peers = lax.axis_size(axis)
    pairs = [(i, i + by) for i in range(peers) if 0 <= i + by < peers]
    return lax.ppermute(value, axis, pairs)


def gathered(value, axis):
    peers = lax.axis_size(axis)
    copies = jnp.broadcast_to(value[None], (peers,) + value.shape)
    return lax.all_to_all(copies, axis, 0, 0, tiled=True)


def summed_over(value, axis, sent_as=jnp.float32):
    peers = lax.axis_size(axis)
    pieces = value.reshape((peers, -1) + value.shape[1:]).astype(sent_as)
    arrived = lax.all_to_all(pieces, axis, 0, 0, tiled=True)
    return arrived.astype(jnp.float32).sum(axis=0)


def reduced_over_dp(value):
    dp_size = lax.axis_size("dp")
    own_piece = summed_over(value.reshape(dp_size, -1), "dp")
    return gathered(own_piece, "dp").reshape(value.shape)


def gelu_tanh(values):
    return jax.nn.gelu(values, approximate=True)


def contract_last(left, right):
    return lax.dot_general(
        left, right, (((1,), (1,)), ((), ())), preferred_element_type=jnp.float32
    )


def neighbours(source, shards_away):
    earlier = passed_along(source, "seq", shards_away)
    later = passed_along(source, "seq", -shards_away)
    return (earlier, later)


def forward_local(
    state, earlier, activated, later, weight, gain_vec, offset_vec, projection, kept_flag
):
    conv_out = jnp.dot(earlier, weight[0], preferred_element_type=jnp.float32)
    conv_out = conv_out + jnp.dot(activated, weight[1], preferred_element_type=jnp.float32)
    conv_out = conv_out + jnp.dot(later, weight[2], preferred_element_type=jnp.float32)
    middle = conv_out * gain_vec + offset_vec
    hidden_act = gelu_tanh(middle).astype(jnp.bfloat16)
    branch = jnp.dot(hidden_act, projection, preferred_element_type=jnp.float32)
    result = (state.astype(jnp.float32) + kept_flag * branch).astype(jnp.bfloat16)
    return (middle, hidden_act, result)


def backward_first(gradient, middle, projection, gain_vec, kept_flag):
    branch_grad = (kept_flag * gradient.astype(jnp.float32)).astype(jnp.bfloat16)
    hidden_grad = contract_last(branch_grad, projection)
    middle_grad = jax.vjp(gelu_tanh, middle)[1](hidden_grad)[0]
    conv_grad = (middle_grad * gain_vec).astype(jnp.bfloat16)
    return (conv_grad, branch_grad)


def backward_second(gradient, earlier, conv_grad, later, weight, normed, gain_vec):
    act_grad = (
        contract_last(later, weight[0])
        + contract_last(conv_grad, weight[1])
        + contract_last(earlier, weight[2])
    )
    normed_grad = jax.vjp(gelu_tanh, normed)[1](act_grad)[0] * gain_vec
    return (gradient.astype(jnp.float32) + normed_grad).astype(jnp.bfloat16)


def grad_rows(hidden_act, branch_grad):
    return lax.dot_general(
        hidden_act, branch_grad, (((0,), (0,)), ((), ())), preferred_element_type=jnp.float32
    )


def exchanged(parts, axis):
    joined = jnp.concatenate(parts, axis=1)
    arrived = lax.all_to_all(joined, axis, 0, 0, tiled=True)
    pieces = []
    offset = 0
    for part in parts:
        pieces.append(arrived[:, offset : offset + part.shape[1]])
        offset += part.shape[1]
    return pieces


def strided_pieces(block, peers):
    return block.reshape(-1, peers, block.shape[-1]).swapaxes(0, 1)


def half_for_each(shard, peers, lanes):
    halves = shard.reshape(2, -1, lanes)
    return jnp.tile(halves, (peers // 2, 1, 1))


def whole_from_halves(own_halves, axis):
    peers = lax.axis_size(axis)
    partner = lax.ppermute(own_halves, axis, [(i, i ^ 1) for i in range(peers)])
    first_core = lax.axis_index(axis) % 2 == 0
    low = jnp.where(first_core, own_halves, partner)
    high = jnp.where(first_core, partner, own_halves)
    return jnp.concatenate([low, high], axis=1)


def conv_from_pieces(pieces, block_shape):
    taps, rows, hidden = block_shape
    parts = pieces.reshape(-1, taps, rows, hidden)
    return jnp.moveaxis(parts, 0, 1).reshape(taps, -1, hidden)


def row_shifted(source, rows_away):
    padding = jnp.zeros((rows_away, source.shape[1]), source.dtype)
    earlier = jnp.concatenate([padding, source[: source.shape[0] - rows_away]], axis=0)
    later = jnp.concatenate([source[rows_away:], padding], axis=0)
    return (earlier, later)


def shards(
    sequence_in,
    output_grad,
    skip_mask,
    in_gain,
    input_shift_vec,
    mid_gain,
    mid_offset,
    conv_weight,
    point_weight,
):
    peers = lax.axis_size("seq")
    channels = sequence_in.shape[2]
    block_shape = conv_weight.shape[1:]
    conv_rows = conv_weight[0].size // channels
    first_weights = jnp.concatenate(
        [conv_weight[0].reshape(-1, channels), point_weight.reshape(-1, channels)]
    )
    state_pieces, first_halves = exchanged(
        [
            strided_pieces(sequence_in[0], peers),
            half_for_each(first_weights, peers, channels),
        ],
        "seq",
    )
    state = state_pieces.reshape(-1, channels)
    grad_in, second_in, state = lax.optimization_barrier((output_grad[0], conv_weight[1], state))
    grad_pieces, second_halves = exchanged(
        [strided_pieces(grad_in, peers), half_for_each(second_in, peers, channels)], "seq"
    )
    first_whole = whole_from_halves(first_halves, "seq")
    first_pieces = first_whole[:, :conv_rows]
    point_full = first_whole[:, conv_rows:].reshape(-1, *point_weight.shape[1:])
    second_pieces = whole_from_halves(second_halves, "seq")
    conv_full = [
        conv_from_pieces(first_pieces, block_shape),
        conv_from_pieces(second_pieces, block_shape),
    ]
    row_reach = (FIRST_DILATION // peers, SECOND_DILATION // peers)
    saved = []
    for block_index in range(2):
        kept_flag = (1 - skip_mask[0, block_index]).astype(jnp.float32)
        normed = state.astype(jnp.float32) * in_gain[block_index] + input_shift_vec[block_index]
        activated = gelu_tanh(normed).astype(jnp.bfloat16)
        earlier, later = row_shifted(activated, row_reach[block_index])
        operands = (
            state,
            earlier,
            activated,
            later,
            conv_full[block_index],
            mid_gain[block_index],
            mid_offset[block_index],
            point_full[:, block_index, :],
            kept_flag,
        )
        middle, hidden_act, state = forward_local(*operands)
        saved.append((normed, middle, hidden_act, kept_flag))
    gradient = grad_pieces.reshape(-1, channels)
    terms = [None, None]
    for block_index in (1, 0):
        normed, middle, hidden_act, kept_flag = saved[block_index]
        projection = point_full[:, block_index, :]
        first_operands = (gradient, middle, projection, mid_gain[block_index], kept_flag)
        conv_grad, branch_grad = backward_first(*first_operands)
        terms[block_index] = grad_rows(hidden_act, branch_grad)
        earlier, later = row_shifted(conv_grad, row_reach[block_index])
        second_operands = (
            gradient,
            earlier,
            conv_grad,
            later,
            conv_full[block_index],
            normed,
            in_gain[block_index],
        )
        gradient = backward_second(*second_operands)
    term_pieces = [
        term.astype(jnp.bfloat16).reshape(peers, -1, channels) for term in terms
    ]
    first_term, second_term, back_pieces = exchanged(
        term_pieces + [gradient.reshape(peers, -1, channels)], "seq"
    )
    own_terms = [
        piece.astype(jnp.float32).sum(axis=0) for piece in (first_term, second_term)
    ]
    summed = reduced_over_dp(jnp.stack(own_terms, axis=1))
    sample_count = sequence_in.shape[0] * lax.axis_size("dp")
    full_length = sequence_in.shape[1] * peers
    point_grad = summed * (1.0 / math.sqrt(sample_count * full_length))
    input_grad = back_pieces.swapaxes(0, 1).reshape(sequence_in.shape)
    return (point_grad, input_grad)


def solution(mesh):
    return jax.shard_map(
        shards,
        mesh=mesh,
        in_specs=(
            P("dp", "seq", None),
            P("dp", "seq", None),
            P("dp", None),
            P(),
            P(),
            P(),
            P(),
            P(None, None, "seq", None),
            P("seq", None, None),
        ),
        out_specs=(P("seq", None, None), P("dp", "seq", None)),
        check_vma=False,
    )
```

```python
import math

import jax
import jax.numpy as jnp
from jax import lax
from jax.sharding import PartitionSpec as P

FIRST_DILATION = 1024
SECOND_DILATION = 2048


def passed_along(value, axis, by):
    peers = lax.axis_size(axis)
    pairs = [(i, i + by) for i in range(peers) if 0 <= i + by < peers]
    return lax.ppermute(value, axis, pairs)


def gathered(value, axis):
    peers = lax.axis_size(axis)
    copies = jnp.broadcast_to(value[None], (peers,) + value.shape)
    return lax.all_to_all(copies, axis, 0, 0, tiled=True)


def summed_over(value, axis, sent_as=jnp.float32):
    peers = lax.axis_size(axis)
    pieces = value.reshape((peers, -1) + value.shape[1:]).astype(sent_as)
    arrived = lax.all_to_all(pieces, axis, 0, 0, tiled=True)
    return arrived.astype(jnp.float32).sum(axis=0)


def reduced_over_dp(value):
    dp_size = lax.axis_size("dp")
    own_piece = summed_over(value.reshape(dp_size, -1), "dp")
    return gathered(own_piece, "dp").reshape(value.shape)


def gelu_tanh(values):
    return jax.nn.gelu(values, approximate=True)


def contract_last(left, right):
    return lax.dot_general(
        left, right, (((1,), (1,)), ((), ())), preferred_element_type=jnp.float32
    )


def neighbours(source, shards_away):
    earlier = passed_along(source, "seq", shards_away)
    later = passed_along(source, "seq", -shards_away)
    return (earlier, later)


def forward_local(
    state, earlier, activated, later, weight, gain_vec, offset_vec, projection, kept_flag
):
    conv_out = jnp.dot(earlier, weight[0], preferred_element_type=jnp.float32)
    conv_out = conv_out + jnp.dot(activated, weight[1], preferred_element_type=jnp.float32)
    conv_out = conv_out + jnp.dot(later, weight[2], preferred_element_type=jnp.float32)
    middle = conv_out * gain_vec + offset_vec
    hidden_act = gelu_tanh(middle).astype(jnp.bfloat16)
    branch = jnp.dot(hidden_act, projection, preferred_element_type=jnp.float32)
    result = (state.astype(jnp.float32) + kept_flag * branch).astype(jnp.bfloat16)
    return (middle, hidden_act, result)


def backward_first(gradient, middle, projection, gain_vec, kept_flag):
    branch_grad = (kept_flag * gradient.astype(jnp.float32)).astype(jnp.bfloat16)
    hidden_grad = contract_last(branch_grad, projection)
    middle_grad = jax.vjp(gelu_tanh, middle)[1](hidden_grad)[0]
    conv_grad = (middle_grad * gain_vec).astype(jnp.bfloat16)
    return (conv_grad, branch_grad)


def backward_second(gradient, earlier, conv_grad, later, weight, normed, gain_vec):
    act_grad = (
        contract_last(later, weight[0])
        + contract_last(conv_grad, weight[1])
        + contract_last(earlier, weight[2])
    )
    normed_grad = jax.vjp(gelu_tanh, normed)[1](act_grad)[0] * gain_vec
    return (gradient.astype(jnp.float32) + normed_grad).astype(jnp.bfloat16)


def grad_rows(hidden_act, branch_grad):
    return lax.dot_general(
        hidden_act, branch_grad, (((0,), (0,)), ((), ())), preferred_element_type=jnp.float32
    )


def exchanged(parts, axis):
    joined = jnp.concatenate(parts, axis=1)
    arrived = lax.all_to_all(joined, axis, 0, 0, tiled=True)
    pieces = []
    offset = 0
    for part in parts:
        pieces.append(arrived[:, offset : offset + part.shape[1]])
        offset += part.shape[1]
    return pieces


def strided_pieces(block, peers):
    return block.reshape(-1, peers, block.shape[-1]).swapaxes(0, 1)


def half_for_each(shard, peers, lanes):
    halves = shard.reshape(2, -1, lanes)
    return jnp.tile(halves, (peers // 2, 1, 1))


def whole_from_halves(own_halves, axis):
    peers = lax.axis_size(axis)
    partner = lax.ppermute(own_halves, axis, [(i, i ^ 1) for i in range(peers)])
    first_core = lax.axis_index(axis) % 2 == 0
    low = jnp.where(first_core, own_halves, partner)
    high = jnp.where(first_core, partner, own_halves)
    return jnp.concatenate([low, high], axis=1)


def conv_from_pieces(pieces, block_shape):
    taps, rows, hidden = block_shape
    parts = pieces.reshape(-1, taps, rows, hidden)
    return jnp.moveaxis(parts, 0, 1).reshape(taps, -1, hidden)


def chip_half(term, peers, channels):
    half = channels // 2
    first_core = lax.axis_index("seq") % 2 == 0
    kept = jnp.where(first_core, term[:, :half], term[:, half:])
    given = jnp.where(first_core, term[:, half:], term[:, :half])
    partner = lax.ppermute(given, "seq", [(i, i ^ 1) for i in range(peers)])
    summed = (kept + partner).astype(jnp.bfloat16)
    return summed.reshape(peers, -1, channels)


def chip_sum(piece, peers, channels):
    half = channels // 2
    parts = piece.reshape(peers // 2, 2, -1, half).astype(jnp.float32).sum(axis=0)
    return jnp.moveaxis(parts, 0, 1).reshape(-1, channels)


def row_shifted(source, rows_away):
    padding = jnp.zeros((rows_away, source.shape[1]), source.dtype)
    earlier = jnp.concatenate([padding, source[: source.shape[0] - rows_away]], axis=0)
    later = jnp.concatenate([source[rows_away:], padding], axis=0)
    return (earlier, later)


def shards(
    sequence_in,
    output_grad,
    skip_mask,
    in_gain,
    input_shift_vec,
    mid_gain,
    mid_offset,
    conv_weight,
    point_weight,
):
    peers = lax.axis_size("seq")
    channels = sequence_in.shape[2]
    block_shape = conv_weight.shape[1:]
    conv_rows = conv_weight[0].size // channels
    first_weights = jnp.concatenate(
        [conv_weight[0].reshape(-1, channels), point_weight.reshape(-1, channels)]
    )
    state_pieces, first_halves = exchanged(
        [
            strided_pieces(sequence_in[0], peers),
            half_for_each(first_weights, peers, channels),
        ],
        "seq",
    )
    state = state_pieces.reshape(-1, channels)
    grad_in, second_in, state = lax.optimization_barrier((output_grad[0], conv_weight[1], state))
    grad_pieces, second_halves = exchanged(
        [strided_pieces(grad_in, peers), half_for_each(second_in, peers, channels)], "seq"
    )
    first_whole = whole_from_halves(first_halves, "seq")
    first_pieces = first_whole[:, :conv_rows]
    point_full = first_whole[:, conv_rows:].reshape(-1, *point_weight.shape[1:])
    second_pieces = whole_from_halves(second_halves, "seq")
    conv_full = [
        conv_from_pieces(first_pieces, block_shape),
        conv_from_pieces(second_pieces, block_shape),
    ]
    row_reach = (FIRST_DILATION // peers, SECOND_DILATION // peers)
    saved = []
    for block_index in range(2):
        kept_flag = (1 - skip_mask[0, block_index]).astype(jnp.float32)
        normed = state.astype(jnp.float32) * in_gain[block_index] + input_shift_vec[block_index]
        activated = gelu_tanh(normed).astype(jnp.bfloat16)
        earlier, later = row_shifted(activated, row_reach[block_index])
        operands = (
            state,
            earlier,
            activated,
            later,
            conv_full[block_index],
            mid_gain[block_index],
            mid_offset[block_index],
            point_full[:, block_index, :],
            kept_flag,
        )
        middle, hidden_act, state = forward_local(*operands)
        saved.append((normed, middle, hidden_act, kept_flag))
    gradient = grad_pieces.reshape(-1, channels)
    terms = [None, None]
    for block_index in (1, 0):
        normed, middle, hidden_act, kept_flag = saved[block_index]
        projection = point_full[:, block_index, :]
        first_operands = (gradient, middle, projection, mid_gain[block_index], kept_flag)
        conv_grad, branch_grad = backward_first(*first_operands)
        terms[block_index] = grad_rows(hidden_act, branch_grad)
        earlier, later = row_shifted(conv_grad, row_reach[block_index])
        second_operands = (
            gradient,
            earlier,
            conv_grad,
            later,
            conv_full[block_index],
            normed,
            in_gain[block_index],
        )
        gradient = backward_second(*second_operands)
    term_pieces = [chip_half(term, peers, channels) for term in terms]
    first_term, second_term, back_pieces = exchanged(
        term_pieces + [gradient.reshape(peers, -1, channels)], "seq"
    )
    own_terms = [chip_sum(piece, peers, channels) for piece in (first_term, second_term)]
    summed = reduced_over_dp(jnp.stack(own_terms, axis=1))
    sample_count = sequence_in.shape[0] * lax.axis_size("dp")
    full_length = sequence_in.shape[1] * peers
    point_grad = summed * (1.0 / math.sqrt(sample_count * full_length))
    input_grad = back_pieces.swapaxes(0, 1).reshape(sequence_in.shape)
    return (point_grad, input_grad)


def solution(mesh):
    return jax.shard_map(
        shards,
        mesh=mesh,
        in_specs=(
            P("dp", "seq", None),
            P("dp", "seq", None),
            P("dp", None),
            P(),
            P(),
            P(),
            P(),
            P(None, None, "seq", None),
            P("seq", None, None),
        ),
        out_specs=(P("seq", None, None), P("dp", "seq", None)),
        check_vma=False,
    )
```

```python
import math

import jax
import jax.numpy as jnp
from jax import lax
from jax.sharding import PartitionSpec as P

FIRST_DILATION = 1024
SECOND_DILATION = 2048


def passed_along(value, axis, by):
    peers = lax.axis_size(axis)
    pairs = [(i, i + by) for i in range(peers) if 0 <= i + by < peers]
    return lax.ppermute(value, axis, pairs)


def gathered(value, axis):
    peers = lax.axis_size(axis)
    copies = jnp.broadcast_to(value[None], (peers,) + value.shape)
    return lax.all_to_all(copies, axis, 0, 0, tiled=True)


def summed_over(value, axis, sent_as=jnp.float32):
    peers = lax.axis_size(axis)
    pieces = value.reshape((peers, -1) + value.shape[1:]).astype(sent_as)
    arrived = lax.all_to_all(pieces, axis, 0, 0, tiled=True)
    return arrived.astype(jnp.float32).sum(axis=0)


def reduced_over_dp(value):
    dp_size = lax.axis_size("dp")
    own_piece = summed_over(value.reshape(dp_size, -1), "dp", jnp.bfloat16)
    return gathered(own_piece, "dp").reshape(value.shape)


def gelu_tanh(values):
    return jax.nn.gelu(values, approximate=True)


def contract_last(left, right):
    return lax.dot_general(
        left, right, (((1,), (1,)), ((), ())), preferred_element_type=jnp.float32
    )


def neighbours(source, shards_away):
    earlier = passed_along(source, "seq", shards_away)
    later = passed_along(source, "seq", -shards_away)
    return (earlier, later)


def forward_local(
    state, earlier, activated, later, weight, gain_vec, offset_vec, projection, kept_flag
):
    conv_out = jnp.dot(earlier, weight[0], preferred_element_type=jnp.float32)
    conv_out = conv_out + jnp.dot(activated, weight[1], preferred_element_type=jnp.float32)
    conv_out = conv_out + jnp.dot(later, weight[2], preferred_element_type=jnp.float32)
    middle = conv_out * gain_vec + offset_vec
    hidden_act = gelu_tanh(middle).astype(jnp.bfloat16)
    branch = jnp.dot(hidden_act, projection, preferred_element_type=jnp.float32)
    result = (state.astype(jnp.float32) + kept_flag * branch).astype(jnp.bfloat16)
    return (middle, hidden_act, result)


def backward_first(gradient, middle, projection, gain_vec, kept_flag):
    branch_grad = (kept_flag * gradient.astype(jnp.float32)).astype(jnp.bfloat16)
    hidden_grad = contract_last(branch_grad, projection)
    middle_grad = jax.vjp(gelu_tanh, middle)[1](hidden_grad)[0]
    conv_grad = (middle_grad * gain_vec).astype(jnp.bfloat16)
    return (conv_grad, branch_grad)


def backward_second(gradient, earlier, conv_grad, later, weight, normed, gain_vec):
    act_grad = (
        contract_last(later, weight[0])
        + contract_last(conv_grad, weight[1])
        + contract_last(earlier, weight[2])
    )
    normed_grad = jax.vjp(gelu_tanh, normed)[1](act_grad)[0] * gain_vec
    return (gradient.astype(jnp.float32) + normed_grad).astype(jnp.bfloat16)


def grad_rows(hidden_act, branch_grad):
    return lax.dot_general(
        hidden_act, branch_grad, (((0,), (0,)), ((), ())), preferred_element_type=jnp.float32
    )


def exchanged(parts, axis):
    joined = jnp.concatenate(parts, axis=1)
    arrived = lax.all_to_all(joined, axis, 0, 0, tiled=True)
    pieces = []
    offset = 0
    for part in parts:
        pieces.append(arrived[:, offset : offset + part.shape[1]])
        offset += part.shape[1]
    return pieces


def strided_pieces(block, peers):
    return block.reshape(-1, peers, block.shape[-1]).swapaxes(0, 1)


def half_for_each(shard, peers, lanes):
    halves = shard.reshape(2, -1, lanes)
    return jnp.tile(halves, (peers // 2, 1, 1))


def whole_from_halves(own_halves, axis):
    peers = lax.axis_size(axis)
    partner = lax.ppermute(own_halves, axis, [(i, i ^ 1) for i in range(peers)])
    first_core = lax.axis_index(axis) % 2 == 0
    low = jnp.where(first_core, own_halves, partner)
    high = jnp.where(first_core, partner, own_halves)
    return jnp.concatenate([low, high], axis=1)


def conv_from_pieces(pieces, block_shape):
    taps, rows, hidden = block_shape
    parts = pieces.reshape(-1, taps, rows, hidden)
    return jnp.moveaxis(parts, 0, 1).reshape(taps, -1, hidden)


def chip_half(term, peers, channels):
    half = channels // 2
    first_core = lax.axis_index("seq") % 2 == 0
    kept = jnp.where(first_core, term[:, :half], term[:, half:])
    given = jnp.where(first_core, term[:, half:], term[:, :half])
    partner = lax.ppermute(given, "seq", [(i, i ^ 1) for i in range(peers)])
    summed = (kept + partner).astype(jnp.bfloat16)
    return summed.reshape(peers, -1, channels)


def chip_sum(piece, peers, channels):
    half = channels // 2
    parts = piece.reshape(peers // 2, 2, -1, half).astype(jnp.float32).sum(axis=0)
    return jnp.moveaxis(parts, 0, 1).reshape(-1, channels)


def row_shifted(source, rows_away):
    padding = jnp.zeros((rows_away, source.shape[1]), source.dtype)
    earlier = jnp.concatenate([padding, source[: source.shape[0] - rows_away]], axis=0)
    later = jnp.concatenate([source[rows_away:], padding], axis=0)
    return (earlier, later)


def shards(
    sequence_in,
    output_grad,
    skip_mask,
    in_gain,
    input_shift_vec,
    mid_gain,
    mid_offset,
    conv_weight,
    point_weight,
):
    peers = lax.axis_size("seq")
    channels = sequence_in.shape[2]
    block_shape = conv_weight.shape[1:]
    conv_rows = conv_weight[0].size // channels
    first_weights = jnp.concatenate(
        [conv_weight[0].reshape(-1, channels), point_weight.reshape(-1, channels)]
    )
    state_pieces, first_halves = exchanged(
        [
            strided_pieces(sequence_in[0], peers),
            half_for_each(first_weights, peers, channels),
        ],
        "seq",
    )
    state = state_pieces.reshape(-1, channels)
    grad_in, second_in, state = lax.optimization_barrier((output_grad[0], conv_weight[1], state))
    grad_pieces, second_halves = exchanged(
        [strided_pieces(grad_in, peers), half_for_each(second_in, peers, channels)], "seq"
    )
    first_whole = whole_from_halves(first_halves, "seq")
    first_pieces = first_whole[:, :conv_rows]
    point_full = first_whole[:, conv_rows:].reshape(-1, *point_weight.shape[1:])
    second_pieces = whole_from_halves(second_halves, "seq")
    conv_full = [
        conv_from_pieces(first_pieces, block_shape),
        conv_from_pieces(second_pieces, block_shape),
    ]
    row_reach = (FIRST_DILATION // peers, SECOND_DILATION // peers)
    saved = []
    for block_index in range(2):
        kept_flag = (1 - skip_mask[0, block_index]).astype(jnp.float32)
        normed = state.astype(jnp.float32) * in_gain[block_index] + input_shift_vec[block_index]
        activated = gelu_tanh(normed).astype(jnp.bfloat16)
        earlier, later = row_shifted(activated, row_reach[block_index])
        operands = (
            state,
            earlier,
            activated,
            later,
            conv_full[block_index],
            mid_gain[block_index],
            mid_offset[block_index],
            point_full[:, block_index, :],
            kept_flag,
        )
        middle, hidden_act, state = forward_local(*operands)
        saved.append((normed, middle, hidden_act, kept_flag))
    gradient = grad_pieces.reshape(-1, channels)
    terms = [None, None]
    for block_index in (1, 0):
        normed, middle, hidden_act, kept_flag = saved[block_index]
        projection = point_full[:, block_index, :]
        first_operands = (gradient, middle, projection, mid_gain[block_index], kept_flag)
        conv_grad, branch_grad = backward_first(*first_operands)
        terms[block_index] = grad_rows(hidden_act, branch_grad)
        earlier, later = row_shifted(conv_grad, row_reach[block_index])
        second_operands = (
            gradient,
            earlier,
            conv_grad,
            later,
            conv_full[block_index],
            normed,
            in_gain[block_index],
        )
        gradient = backward_second(*second_operands)
    term_pieces = [chip_half(term, peers, channels) for term in terms]
    first_term, second_term, back_pieces = exchanged(
        term_pieces + [gradient.reshape(peers, -1, channels)], "seq"
    )
    own_terms = [chip_sum(piece, peers, channels) for piece in (first_term, second_term)]
    summed = reduced_over_dp(jnp.stack(own_terms, axis=1))
    sample_count = sequence_in.shape[0] * lax.axis_size("dp")
    full_length = sequence_in.shape[1] * peers
    point_grad = summed * (1.0 / math.sqrt(sample_count * full_length))
    input_grad = back_pieces.swapaxes(0, 1).reshape(sequence_in.shape)
    return (point_grad, input_grad)


def solution(mesh):
    return jax.shard_map(
        shards,
        mesh=mesh,
        in_specs=(
            P("dp", "seq", None),
            P("dp", "seq", None),
            P("dp", None),
            P(),
            P(),
            P(),
            P(),
            P(None, None, "seq", None),
            P("seq", None, None),
        ),
        out_specs=(P("seq", None, None), P("dp", "seq", None)),
        check_vma=False,
    )
```

```python
import math

import jax
import jax.numpy as jnp
from jax import lax
from jax.sharding import PartitionSpec as P

FIRST_DILATION = 1024
SECOND_DILATION = 2048


def passed_along(value, axis, by):
    peers = lax.axis_size(axis)
    pairs = [(i, i + by) for i in range(peers) if 0 <= i + by < peers]
    return lax.ppermute(value, axis, pairs)


def gathered(value, axis):
    peers = lax.axis_size(axis)
    copies = jnp.broadcast_to(value[None], (peers,) + value.shape)
    return lax.all_to_all(copies, axis, 0, 0, tiled=True)


def summed_over(value, axis, sent_as=jnp.float32):
    peers = lax.axis_size(axis)
    pieces = value.reshape((peers, -1) + value.shape[1:]).astype(sent_as)
    arrived = lax.all_to_all(pieces, axis, 0, 0, tiled=True)
    return arrived.astype(jnp.float32).sum(axis=0)


def reduced_over_dp(value):
    dp_size = lax.axis_size("dp")
    own_piece = summed_over(value.reshape(dp_size, -1), "dp", jnp.bfloat16)
    return gathered(own_piece, "dp").reshape(value.shape)


def gelu_tanh(values):
    return jax.nn.gelu(values, approximate=True)


def contract_last(left, right):
    return lax.dot_general(
        left, right, (((1,), (1,)), ((), ())), preferred_element_type=jnp.float32
    )


def neighbours(source, shards_away):
    earlier = passed_along(source, "seq", shards_away)
    later = passed_along(source, "seq", -shards_away)
    return (earlier, later)


def forward_local(
    state, earlier, activated, later, weight, gain_vec, offset_vec, projection, kept_flag
):
    conv_out = jnp.dot(earlier, weight[0], preferred_element_type=jnp.float32)
    conv_out = conv_out + jnp.dot(activated, weight[1], preferred_element_type=jnp.float32)
    conv_out = conv_out + jnp.dot(later, weight[2], preferred_element_type=jnp.float32)
    middle = conv_out * gain_vec + offset_vec
    hidden_act = gelu_tanh(middle).astype(jnp.bfloat16)
    branch = jnp.dot(hidden_act, projection, preferred_element_type=jnp.float32)
    result = (state.astype(jnp.float32) + kept_flag * branch).astype(jnp.bfloat16)
    return (middle, hidden_act, result)


def backward_first(gradient, middle, projection, gain_vec, kept_flag):
    branch_grad = (kept_flag * gradient.astype(jnp.float32)).astype(jnp.bfloat16)
    hidden_grad = contract_last(branch_grad, projection)
    middle_grad = jax.vjp(gelu_tanh, middle)[1](hidden_grad)[0]
    conv_grad = (middle_grad * gain_vec).astype(jnp.bfloat16)
    return (conv_grad, branch_grad)


def backward_second(gradient, earlier, conv_grad, later, weight, normed, gain_vec):
    act_grad = (
        contract_last(later, weight[0])
        + contract_last(conv_grad, weight[1])
        + contract_last(earlier, weight[2])
    )
    normed_grad = jax.vjp(gelu_tanh, normed)[1](act_grad)[0] * gain_vec
    return (gradient.astype(jnp.float32) + normed_grad).astype(jnp.bfloat16)


def grad_rows(hidden_act, branch_grad):
    return lax.dot_general(
        hidden_act, branch_grad, (((0,), (0,)), ((), ())), preferred_element_type=jnp.float32
    )


def exchanged(parts, axis):
    joined = jnp.concatenate(parts, axis=1)
    arrived = lax.all_to_all(joined, axis, 0, 0, tiled=True)
    pieces = []
    offset = 0
    for part in parts:
        pieces.append(arrived[:, offset : offset + part.shape[1]])
        offset += part.shape[1]
    return pieces


def strided_pieces(block, peers):
    return block.reshape(-1, peers, block.shape[-1]).swapaxes(0, 1)


def half_for_each(shard, peers, lanes):
    halves = shard.reshape(2, -1, lanes)
    return jnp.tile(halves, (peers // 2, 1, 1))


def whole_from_halves(own_halves, axis):
    peers = lax.axis_size(axis)
    partner = lax.ppermute(own_halves, axis, [(i, i ^ 1) for i in range(peers)])
    first_core = lax.axis_index(axis) % 2 == 0
    low = jnp.where(first_core, own_halves, partner)
    high = jnp.where(first_core, partner, own_halves)
    return jnp.concatenate([low, high], axis=1)


def conv_from_pieces(pieces, block_shape):
    taps, rows, hidden = block_shape
    parts = pieces.reshape(-1, taps, rows, hidden)
    return jnp.moveaxis(parts, 0, 1).reshape(taps, -1, hidden)


def chip_half(term, peers, channels):
    half = channels // 2
    first_core = lax.axis_index("seq") % 2 == 0
    kept = jnp.where(first_core, term[:, :half], term[:, half:])
    given = jnp.where(first_core, term[:, half:], term[:, :half])
    partner = lax.ppermute(given, "seq", [(i, i ^ 1) for i in range(peers)])
    summed = (kept + partner).astype(jnp.bfloat16)
    return summed.reshape(peers, -1, channels)


def chip_sum(piece, peers, channels):
    half = channels // 2
    parts = piece.reshape(peers // 2, 2, -1, half).astype(jnp.float32).sum(axis=0)
    return jnp.moveaxis(parts, 0, 1).reshape(-1, channels)


def row_shifted(source, rows_away):
    padding = jnp.zeros((rows_away, source.shape[1]), source.dtype)
    earlier = jnp.concatenate([padding, source[: source.shape[0] - rows_away]], axis=0)
    later = jnp.concatenate([source[rows_away:], padding], axis=0)
    return (earlier, later)


def shards(
    sequence_in,
    output_grad,
    skip_mask,
    in_gain,
    input_shift_vec,
    mid_gain,
    mid_offset,
    conv_weight,
    point_weight,
):
    peers = lax.axis_size("seq")
    channels = sequence_in.shape[2]
    block_shape = conv_weight.shape[1:]
    conv_rows = conv_weight[0].size // channels
    point_rows = point_weight.size // channels
    all_weights = jnp.concatenate(
        [
            conv_weight[0].reshape(-1, channels),
            point_weight.reshape(-1, channels),
            conv_weight[1].reshape(-1, channels),
        ]
    )
    state_pieces, grad_pieces, weight_halves = exchanged(
        [
            strided_pieces(sequence_in[0], peers),
            strided_pieces(output_grad[0], peers),
            half_for_each(all_weights, peers, channels),
        ],
        "seq",
    )
    state = state_pieces.reshape(-1, channels)
    weight_whole = whole_from_halves(weight_halves, "seq")
    first_pieces = weight_whole[:, :conv_rows]
    point_full = weight_whole[:, conv_rows : conv_rows + point_rows].reshape(
        -1, *point_weight.shape[1:]
    )
    second_pieces = weight_whole[:, conv_rows + point_rows :]
    conv_full = [
        conv_from_pieces(first_pieces, block_shape),
        conv_from_pieces(second_pieces, block_shape),
    ]
    row_reach = (FIRST_DILATION // peers, SECOND_DILATION // peers)
    saved = []
    for block_index in range(2):
        kept_flag = (1 - skip_mask[0, block_index]).astype(jnp.float32)
        normed = state.astype(jnp.float32) * in_gain[block_index] + input_shift_vec[block_index]
        activated = gelu_tanh(normed).astype(jnp.bfloat16)
        earlier, later = row_shifted(activated, row_reach[block_index])
        operands = (
            state,
            earlier,
            activated,
            later,
            conv_full[block_index],
            mid_gain[block_index],
            mid_offset[block_index],
            point_full[:, block_index, :],
            kept_flag,
        )
        middle, hidden_act, state = forward_local(*operands)
        saved.append((normed, middle, hidden_act, kept_flag))
    gradient = grad_pieces.reshape(-1, channels)
    terms = [None, None]
    for block_index in (1, 0):
        normed, middle, hidden_act, kept_flag = saved[block_index]
        projection = point_full[:, block_index, :]
        first_operands = (gradient, middle, projection, mid_gain[block_index], kept_flag)
        conv_grad, branch_grad = backward_first(*first_operands)
        terms[block_index] = grad_rows(hidden_act, branch_grad)
        earlier, later = row_shifted(conv_grad, row_reach[block_index])
        second_operands = (
            gradient,
            earlier,
            conv_grad,
            later,
            conv_full[block_index],
            normed,
            in_gain[block_index],
        )
        gradient = backward_second(*second_operands)
    term_pieces = [chip_half(term, peers, channels) for term in terms]
    first_term, second_term, back_pieces = exchanged(
        term_pieces + [gradient.reshape(peers, -1, channels)], "seq"
    )
    own_terms = [chip_sum(piece, peers, channels) for piece in (first_term, second_term)]
    summed = reduced_over_dp(jnp.stack(own_terms, axis=1))
    sample_count = sequence_in.shape[0] * lax.axis_size("dp")
    full_length = sequence_in.shape[1] * peers
    point_grad = summed * (1.0 / math.sqrt(sample_count * full_length))
    input_grad = back_pieces.swapaxes(0, 1).reshape(sequence_in.shape)
    return (point_grad, input_grad)


def solution(mesh):
    return jax.shard_map(
        shards,
        mesh=mesh,
        in_specs=(
            P("dp", "seq", None),
            P("dp", "seq", None),
            P("dp", None),
            P(),
            P(),
            P(),
            P(),
            P(None, None, "seq", None),
            P("seq", None, None),
        ),
        out_specs=(P("seq", None, None), P("dp", "seq", None)),
        check_vma=False,
    )
```

```python
import math

import jax
import jax.numpy as jnp
from jax import lax
from jax.sharding import PartitionSpec as P

FIRST_DILATION = 1024
SECOND_DILATION = 2048


def passed_along(value, axis, by):
    peers = lax.axis_size(axis)
    pairs = [(i, i + by) for i in range(peers) if 0 <= i + by < peers]
    return lax.ppermute(value, axis, pairs)


def gathered(value, axis):
    peers = lax.axis_size(axis)
    copies = jnp.broadcast_to(value[None], (peers,) + value.shape)
    return lax.all_to_all(copies, axis, 0, 0, tiled=True)


def summed_over(value, axis, sent_as=jnp.float32):
    peers = lax.axis_size(axis)
    pieces = value.reshape((peers, -1) + value.shape[1:]).astype(sent_as)
    arrived = lax.all_to_all(pieces, axis, 0, 0, tiled=True)
    return arrived.astype(jnp.float32).sum(axis=0)


def reduced_over_dp(value):
    dp_size = lax.axis_size("dp")
    own_piece = summed_over(value.reshape(dp_size, -1), "dp", jnp.bfloat16)
    return gathered(own_piece, "dp").reshape(value.shape)


def gelu_tanh(values):
    return jax.nn.gelu(values, approximate=True)


def contract_last(left, right):
    return lax.dot_general(
        left, right, (((1,), (1,)), ((), ())), preferred_element_type=jnp.float32
    )


def neighbours(source, shards_away):
    earlier = passed_along(source, "seq", shards_away)
    later = passed_along(source, "seq", -shards_away)
    return (earlier, later)


def forward_local(
    state, earlier, activated, later, weight, gain_vec, offset_vec, projection, kept_flag
):
    conv_out = jnp.dot(earlier, weight[0], preferred_element_type=jnp.float32)
    conv_out = conv_out + jnp.dot(activated, weight[1], preferred_element_type=jnp.float32)
    conv_out = conv_out + jnp.dot(later, weight[2], preferred_element_type=jnp.float32)
    middle = conv_out * gain_vec + offset_vec
    hidden_act = gelu_tanh(middle).astype(jnp.bfloat16)
    branch = jnp.dot(hidden_act, projection, preferred_element_type=jnp.float32)
    result = (state.astype(jnp.float32) + kept_flag * branch).astype(jnp.bfloat16)
    return (middle, hidden_act, result)


def backward_first(gradient, middle, projection, gain_vec, kept_flag):
    branch_grad = (kept_flag * gradient.astype(jnp.float32)).astype(jnp.bfloat16)
    hidden_grad = contract_last(branch_grad, projection)
    middle_grad = jax.vjp(gelu_tanh, middle)[1](hidden_grad)[0]
    conv_grad = (middle_grad * gain_vec).astype(jnp.bfloat16)
    return (conv_grad, branch_grad)


def backward_second(gradient, earlier, conv_grad, later, weight, normed, gain_vec):
    act_grad = (
        contract_last(later, weight[0])
        + contract_last(conv_grad, weight[1])
        + contract_last(earlier, weight[2])
    )
    normed_grad = jax.vjp(gelu_tanh, normed)[1](act_grad)[0] * gain_vec
    return (gradient.astype(jnp.float32) + normed_grad).astype(jnp.bfloat16)


def grad_rows(hidden_act, branch_grad):
    return lax.dot_general(
        hidden_act, branch_grad, (((0,), (0,)), ((), ())), preferred_element_type=jnp.float32
    )


def exchanged(parts, axis):
    joined = jnp.concatenate(parts, axis=1)
    arrived = lax.all_to_all(joined, axis, 0, 0, tiled=True)
    pieces = []
    offset = 0
    for part in parts:
        pieces.append(arrived[:, offset : offset + part.shape[1]])
        offset += part.shape[1]
    return pieces


def strided_pieces(block, peers):
    return block.reshape(-1, peers, block.shape[-1]).swapaxes(0, 1)


def half_for_each(shard, peers, lanes):
    halves = shard.reshape(2, -1, lanes)
    return jnp.tile(halves, (peers // 2, 1, 1))


def whole_from_halves(own_halves, axis):
    peers = lax.axis_size(axis)
    partner = lax.ppermute(own_halves, axis, [(i, i ^ 1) for i in range(peers)])
    first_core = lax.axis_index(axis) % 2 == 0
    low = jnp.where(first_core, own_halves, partner)
    high = jnp.where(first_core, partner, own_halves)
    return jnp.concatenate([low, high], axis=1)


def conv_from_pieces(pieces, block_shape):
    taps, rows, hidden = block_shape
    parts = pieces.reshape(-1, taps, rows, hidden)
    return jnp.moveaxis(parts, 0, 1).reshape(taps, -1, hidden)


def chip_half(term, peers, channels):
    half = channels // 2
    first_core = lax.axis_index("seq") % 2 == 0
    kept = jnp.where(first_core, term[:, :half], term[:, half:])
    given = jnp.where(first_core, term[:, half:], term[:, :half])
    partner = lax.ppermute(given, "seq", [(i, i ^ 1) for i in range(peers)])
    summed = (kept + partner).astype(jnp.bfloat16)
    return summed.reshape(peers, -1, channels)


def chip_sum(piece, peers, channels):
    half = channels // 2
    parts = piece.reshape(peers // 2, 2, -1, half).astype(jnp.float32).sum(axis=0)
    return jnp.moveaxis(parts, 0, 1).reshape(-1, channels)


def row_shifted(source, rows_away):
    padding = jnp.zeros((rows_away, source.shape[1]), source.dtype)
    earlier = jnp.concatenate([padding, source[: source.shape[0] - rows_away]], axis=0)
    later = jnp.concatenate([source[rows_away:], padding], axis=0)
    return (earlier, later)


def shards(
    sequence_in,
    output_grad,
    skip_mask,
    in_gain,
    input_shift_vec,
    mid_gain,
    mid_offset,
    conv_weight,
    point_weight,
):
    peers = lax.axis_size("seq")
    channels = sequence_in.shape[2]
    block_shape = conv_weight.shape[1:]
    conv_rows = conv_weight[0].size // channels
    first_weights = jnp.concatenate(
        [conv_weight[0].reshape(-1, channels), point_weight.reshape(-1, channels)]
    )
    state_pieces, first_halves = exchanged(
        [
            strided_pieces(sequence_in[0], peers),
            half_for_each(first_weights, peers, channels),
        ],
        "seq",
    )
    state = state_pieces.reshape(-1, channels)
    grad_in, second_in, state = lax.optimization_barrier((output_grad[0], conv_weight[1], state))
    grad_pieces, second_halves = exchanged(
        [strided_pieces(grad_in, peers), half_for_each(second_in, peers, channels)], "seq"
    )
    first_whole = whole_from_halves(first_halves, "seq")
    first_pieces = first_whole[:, :conv_rows]
    point_full = first_whole[:, conv_rows:].reshape(-1, *point_weight.shape[1:])
    second_pieces = whole_from_halves(second_halves, "seq")
    conv_full = [
        conv_from_pieces(first_pieces, block_shape),
        conv_from_pieces(second_pieces, block_shape),
    ]
    row_reach = (FIRST_DILATION // peers, SECOND_DILATION // peers)
    saved = []
    for block_index in range(2):
        kept_flag = (1 - skip_mask[0, block_index]).astype(jnp.float32)
        normed = state.astype(jnp.float32) * in_gain[block_index] + input_shift_vec[block_index]
        activated = gelu_tanh(normed).astype(jnp.bfloat16)
        earlier, later = row_shifted(activated, row_reach[block_index])
        operands = (
            state,
            earlier,
            activated,
            later,
            conv_full[block_index],
            mid_gain[block_index],
            mid_offset[block_index],
            point_full[:, block_index, :],
            kept_flag,
        )
        middle, hidden_act, state = forward_local(*operands)
        saved.append((normed, middle, hidden_act, kept_flag))
    gradient = grad_pieces.reshape(-1, channels)
    terms = [None, None]
    for block_index in (1, 0):
        normed, middle, hidden_act, kept_flag = saved[block_index]
        projection = point_full[:, block_index, :]
        first_operands = (gradient, middle, projection, mid_gain[block_index], kept_flag)
        conv_grad, branch_grad = backward_first(*first_operands)
        terms[block_index] = chip_half(grad_rows(hidden_act, branch_grad), peers, channels)
        earlier, later = row_shifted(conv_grad, row_reach[block_index])
        second_operands = (
            gradient,
            earlier,
            conv_grad,
            later,
            conv_full[block_index],
            normed,
            in_gain[block_index],
        )
        gradient = backward_second(*second_operands)
        if block_index == 1:
            terms[1], gradient = lax.optimization_barrier((terms[1], gradient))
    first_term, second_term, back_pieces = exchanged(
        terms + [gradient.reshape(peers, -1, channels)], "seq"
    )
    own_terms = [chip_sum(piece, peers, channels) for piece in (first_term, second_term)]
    summed = reduced_over_dp(jnp.stack(own_terms, axis=1))
    sample_count = sequence_in.shape[0] * lax.axis_size("dp")
    full_length = sequence_in.shape[1] * peers
    point_grad = summed * (1.0 / math.sqrt(sample_count * full_length))
    input_grad = back_pieces.swapaxes(0, 1).reshape(sequence_in.shape)
    return (point_grad, input_grad)


def solution(mesh):
    return jax.shard_map(
        shards,
        mesh=mesh,
        in_specs=(
            P("dp", "seq", None),
            P("dp", "seq", None),
            P("dp", None),
            P(),
            P(),
            P(),
            P(),
            P(None, None, "seq", None),
            P("seq", None, None),
        ),
        out_specs=(P("seq", None, None), P("dp", "seq", None)),
        check_vma=False,
    )
```

```python
import math

import jax
import jax.numpy as jnp
from jax import lax
from jax.sharding import PartitionSpec as P

FIRST_DILATION = 1024
SECOND_DILATION = 2048


def passed_along(value, axis, by):
    peers = lax.axis_size(axis)
    pairs = [(i, i + by) for i in range(peers) if 0 <= i + by < peers]
    return lax.ppermute(value, axis, pairs)


def gathered(value, axis):
    peers = lax.axis_size(axis)
    copies = jnp.broadcast_to(value[None], (peers,) + value.shape)
    return lax.all_to_all(copies, axis, 0, 0, tiled=True)


def summed_over(value, axis, sent_as=jnp.float32):
    peers = lax.axis_size(axis)
    pieces = value.reshape((peers, -1) + value.shape[1:]).astype(sent_as)
    arrived = lax.all_to_all(pieces, axis, 0, 0, tiled=True)
    return arrived.astype(jnp.float32).sum(axis=0)


def reduced_over_dp(value):
    dp_size = lax.axis_size("dp")
    own_piece = summed_over(value.reshape(dp_size, -1), "dp", jnp.bfloat16)
    return gathered(own_piece, "dp").reshape(value.shape)


def gelu_tanh(values):
    return jax.nn.gelu(values, approximate=True)


def contract_last(left, right):
    return lax.dot_general(
        left, right, (((1,), (1,)), ((), ())), preferred_element_type=jnp.float32
    )


def neighbours(source, shards_away):
    earlier = passed_along(source, "seq", shards_away)
    later = passed_along(source, "seq", -shards_away)
    return (earlier, later)


def forward_local(
    state, earlier, activated, later, weight, gain_vec, offset_vec, projection, kept_flag
):
    conv_out = jnp.dot(earlier, weight[0], preferred_element_type=jnp.float32)
    conv_out = conv_out + jnp.dot(activated, weight[1], preferred_element_type=jnp.float32)
    conv_out = conv_out + jnp.dot(later, weight[2], preferred_element_type=jnp.float32)
    middle = conv_out * gain_vec + offset_vec
    hidden_act = gelu_tanh(middle).astype(jnp.bfloat16)
    branch = jnp.dot(hidden_act, projection, preferred_element_type=jnp.float32)
    result = (state.astype(jnp.float32) + kept_flag * branch).astype(jnp.bfloat16)
    return (middle, hidden_act, result)


def backward_first(gradient, middle, projection, gain_vec, kept_flag):
    branch_grad = (kept_flag * gradient.astype(jnp.float32)).astype(jnp.bfloat16)
    hidden_grad = contract_last(branch_grad, projection)
    middle_grad = jax.vjp(gelu_tanh, middle)[1](hidden_grad)[0]
    conv_grad = (middle_grad * gain_vec).astype(jnp.bfloat16)
    return (conv_grad, branch_grad)


def backward_second(gradient, earlier, conv_grad, later, weight, normed, gain_vec):
    act_grad = (
        contract_last(later, weight[0])
        + contract_last(conv_grad, weight[1])
        + contract_last(earlier, weight[2])
    )
    normed_grad = jax.vjp(gelu_tanh, normed)[1](act_grad)[0] * gain_vec
    return (gradient.astype(jnp.float32) + normed_grad).astype(jnp.bfloat16)


def grad_rows(hidden_act, branch_grad):
    return lax.dot_general(
        hidden_act, branch_grad, (((0,), (0,)), ((), ())), preferred_element_type=jnp.float32
    )


def exchanged(parts, axis):
    joined = jnp.concatenate(parts, axis=1)
    arrived = lax.all_to_all(joined, axis, 0, 0, tiled=True)
    pieces = []
    offset = 0
    for part in parts:
        pieces.append(arrived[:, offset : offset + part.shape[1]])
        offset += part.shape[1]
    return pieces


def strided_pieces(block, peers):
    return block.reshape(peers, -1, block.shape[-1])


def half_for_each(shard, peers, lanes):
    halves = shard.reshape(2, -1, lanes)
    return jnp.tile(halves, (peers // 2, 1, 1))


def whole_from_halves(own_halves, axis):
    peers = lax.axis_size(axis)
    partner = lax.ppermute(own_halves, axis, [(i, i ^ 1) for i in range(peers)])
    first_core = lax.axis_index(axis) % 2 == 0
    low = jnp.where(first_core, own_halves, partner)
    high = jnp.where(first_core, partner, own_halves)
    return jnp.concatenate([low, high], axis=1)


def conv_from_pieces(pieces, block_shape):
    taps, rows, hidden = block_shape
    parts = pieces.reshape(-1, taps, rows, hidden)
    return jnp.moveaxis(parts, 0, 1).reshape(taps, -1, hidden)


def chip_half(term, peers, channels):
    half = channels // 2
    first_core = lax.axis_index("seq") % 2 == 0
    kept = jnp.where(first_core, term[:, :half], term[:, half:])
    given = jnp.where(first_core, term[:, half:], term[:, :half])
    partner = lax.ppermute(given, "seq", [(i, i ^ 1) for i in range(peers)])
    summed = (kept + partner).astype(jnp.bfloat16)
    return summed.reshape(peers, -1, channels)


def chip_sum(piece, peers, channels):
    half = channels // 2
    parts = piece.reshape(peers // 2, 2, -1, half).astype(jnp.float32).sum(axis=0)
    return jnp.moveaxis(parts, 0, 1).reshape(-1, channels)


def row_shifted(source, rows_away):
    padding = jnp.zeros((rows_away, source.shape[1]), source.dtype)
    earlier = jnp.concatenate([padding, source[: source.shape[0] - rows_away]], axis=0)
    later = jnp.concatenate([source[rows_away:], padding], axis=0)
    return (earlier, later)


def shards(
    sequence_in,
    output_grad,
    skip_mask,
    in_gain,
    input_shift_vec,
    mid_gain,
    mid_offset,
    conv_weight,
    point_weight,
):
    peers = lax.axis_size("seq")
    channels = sequence_in.shape[2]
    block_shape = conv_weight.shape[1:]
    conv_rows = conv_weight[0].size // channels
    first_weights = jnp.concatenate(
        [conv_weight[0].reshape(-1, channels), point_weight.reshape(-1, channels)]
    )
    state_pieces, first_halves = exchanged(
        [
            strided_pieces(sequence_in[0], peers),
            half_for_each(first_weights, peers, channels),
        ],
        "seq",
    )
    state = state_pieces.reshape(-1, channels)
    grad_in, second_in, state = lax.optimization_barrier((output_grad[0], conv_weight[1], state))
    grad_pieces, second_halves = exchanged(
        [strided_pieces(grad_in, peers), half_for_each(second_in, peers, channels)], "seq"
    )
    first_whole = whole_from_halves(first_halves, "seq")
    first_pieces = first_whole[:, :conv_rows]
    point_full = first_whole[:, conv_rows:].reshape(-1, *point_weight.shape[1:])
    second_pieces = whole_from_halves(second_halves, "seq")
    conv_full = [
        conv_from_pieces(first_pieces, block_shape),
        conv_from_pieces(second_pieces, block_shape),
    ]
    row_reach = (FIRST_DILATION // peers, SECOND_DILATION // peers)
    saved = []
    for block_index in range(2):
        kept_flag = (1 - skip_mask[0, block_index]).astype(jnp.float32)
        normed = state.astype(jnp.float32) * in_gain[block_index] + input_shift_vec[block_index]
        activated = gelu_tanh(normed).astype(jnp.bfloat16)
        earlier, later = row_shifted(activated, row_reach[block_index])
        operands = (
            state,
            earlier,
            activated,
            later,
            conv_full[block_index],
            mid_gain[block_index],
            mid_offset[block_index],
            point_full[:, block_index, :],
            kept_flag,
        )
        middle, hidden_act, state = forward_local(*operands)
        saved.append((normed, middle, hidden_act, kept_flag))
    gradient = grad_pieces.reshape(-1, channels)
    terms = [None, None]
    for block_index in (1, 0):
        normed, middle, hidden_act, kept_flag = saved[block_index]
        projection = point_full[:, block_index, :]
        first_operands = (gradient, middle, projection, mid_gain[block_index], kept_flag)
        conv_grad, branch_grad = backward_first(*first_operands)
        terms[block_index] = chip_half(grad_rows(hidden_act, branch_grad), peers, channels)
        earlier, later = row_shifted(conv_grad, row_reach[block_index])
        second_operands = (
            gradient,
            earlier,
            conv_grad,
            later,
            conv_full[block_index],
            normed,
            in_gain[block_index],
        )
        gradient = backward_second(*second_operands)
        if block_index == 1:
            terms[1], gradient = lax.optimization_barrier((terms[1], gradient))
    first_term, second_term, back_pieces = exchanged(
        terms + [gradient.reshape(peers, -1, channels)], "seq"
    )
    own_terms = [chip_sum(piece, peers, channels) for piece in (first_term, second_term)]
    summed = reduced_over_dp(jnp.stack(own_terms, axis=1))
    sample_count = sequence_in.shape[0] * lax.axis_size("dp")
    full_length = sequence_in.shape[1] * peers
    point_grad = summed * (1.0 / math.sqrt(sample_count * full_length))
    input_grad = back_pieces.reshape(sequence_in.shape)
    return (point_grad, input_grad)


def solution(mesh):
    return jax.shard_map(
        shards,
        mesh=mesh,
        in_specs=(
            P("dp", "seq", None),
            P("dp", "seq", None),
            P("dp", None),
            P(),
            P(),
            P(),
            P(),
            P(None, None, "seq", None),
            P("seq", None, None),
        ),
        out_specs=(P("seq", None, None), P("dp", "seq", None)),
        check_vma=False,
    )
```

```python
import math

import jax
import jax.numpy as jnp
from jax import lax
from jax.sharding import PartitionSpec as P

FIRST_DILATION = 1024
SECOND_DILATION = 2048


def passed_along(value, axis, by):
    peers = lax.axis_size(axis)
    pairs = [(i, i + by) for i in range(peers) if 0 <= i + by < peers]
    return lax.ppermute(value, axis, pairs)


def gathered(value, axis):
    peers = lax.axis_size(axis)
    copies = jnp.broadcast_to(value[None], (peers,) + value.shape)
    return lax.all_to_all(copies, axis, 0, 0, tiled=True)


def summed_over(value, axis, sent_as=jnp.float32):
    peers = lax.axis_size(axis)
    pieces = value.reshape((peers, -1) + value.shape[1:]).astype(sent_as)
    arrived = lax.all_to_all(pieces, axis, 0, 0, tiled=True)
    return arrived.astype(jnp.float32).sum(axis=0)


def reduced_over_dp(value):
    dp_size = lax.axis_size("dp")
    own_piece = summed_over(value.reshape(dp_size, -1), "dp", jnp.bfloat16)
    return gathered(own_piece, "dp").reshape(value.shape)


def gelu_tanh(values):
    return jax.nn.gelu(values, approximate=True)


def contract_last(left, right):
    return lax.dot_general(
        left, right, (((1,), (1,)), ((), ())), preferred_element_type=jnp.float32
    )


def neighbours(source, shards_away):
    earlier = passed_along(source, "seq", shards_away)
    later = passed_along(source, "seq", -shards_away)
    return (earlier, later)


def forward_local(
    state, earlier, activated, later, weight, gain_vec, offset_vec, projection, kept_flag
):
    conv_out = jnp.dot(earlier, weight[0], preferred_element_type=jnp.float32)
    conv_out = conv_out + jnp.dot(activated, weight[1], preferred_element_type=jnp.float32)
    conv_out = conv_out + jnp.dot(later, weight[2], preferred_element_type=jnp.float32)
    middle = conv_out * gain_vec + offset_vec
    hidden_act = gelu_tanh(middle).astype(jnp.bfloat16)
    branch = jnp.dot(hidden_act, projection, preferred_element_type=jnp.float32)
    result = (state.astype(jnp.float32) + kept_flag * branch).astype(jnp.bfloat16)
    return (middle, hidden_act, result)


def backward_first(gradient, middle, projection, gain_vec, kept_flag):
    branch_grad = (kept_flag * gradient.astype(jnp.float32)).astype(jnp.bfloat16)
    hidden_grad = contract_last(branch_grad, projection)
    middle_grad = jax.vjp(gelu_tanh, middle)[1](hidden_grad)[0]
    conv_grad = (middle_grad * gain_vec).astype(jnp.bfloat16)
    return (conv_grad, branch_grad)


def backward_second(gradient, earlier, conv_grad, later, weight, normed, gain_vec):
    act_grad = (
        contract_last(later, weight[0])
        + contract_last(conv_grad, weight[1])
        + contract_last(earlier, weight[2])
    )
    normed_grad = jax.vjp(gelu_tanh, normed)[1](act_grad)[0] * gain_vec
    return (gradient.astype(jnp.float32) + normed_grad).astype(jnp.bfloat16)


def grad_rows(hidden_act, branch_grad):
    return lax.dot_general(
        hidden_act, branch_grad, (((0,), (0,)), ((), ())), preferred_element_type=jnp.float32
    )


def exchanged(parts, axis):
    joined = jnp.concatenate(parts, axis=1)
    arrived = lax.all_to_all(joined, axis, 0, 0, tiled=True)
    pieces = []
    offset = 0
    for part in parts:
        pieces.append(arrived[:, offset : offset + part.shape[1]])
        offset += part.shape[1]
    return pieces


def strided_pieces(block, peers):
    return block.reshape(peers, -1, block.shape[-1])


def half_for_each(shard, peers, lanes):
    halves = shard.reshape(2, -1, lanes)
    return jnp.tile(halves, (peers // 2, 1, 1))


def whole_from_halves(own_halves, axis):
    peers = lax.axis_size(axis)
    partner = lax.ppermute(own_halves, axis, [(i, i ^ 1) for i in range(peers)])
    first_core = lax.axis_index(axis) % 2 == 0
    low = jnp.where(first_core, own_halves, partner)
    high = jnp.where(first_core, partner, own_halves)
    return jnp.concatenate([low, high], axis=1)


def conv_from_pieces(pieces, block_shape):
    taps, rows, hidden = block_shape
    parts = pieces.reshape(-1, taps, rows, hidden)
    return jnp.moveaxis(parts, 0, 1).reshape(taps, -1, hidden)


def chip_half(term, peers, channels):
    half = channels // 2
    first_core = lax.axis_index("seq") % 2 == 0
    kept = jnp.where(first_core, term[:, :half], term[:, half:])
    given = jnp.where(first_core, term[:, half:], term[:, :half])
    partner = lax.ppermute(given, "seq", [(i, i ^ 1) for i in range(peers)])
    summed = (kept + partner).astype(jnp.bfloat16)
    return summed.reshape(peers, -1, channels)


def chip_sum(piece, peers, channels):
    half = channels // 2
    parts = piece.reshape(peers // 2, 2, -1, half).astype(jnp.float32).sum(axis=0)
    return jnp.moveaxis(parts, 0, 1).reshape(-1, channels)


def row_shifted(source, rows_away):
    padding = jnp.zeros((rows_away, source.shape[1]), source.dtype)
    earlier = jnp.concatenate([padding, source[: source.shape[0] - rows_away]], axis=0)
    later = jnp.concatenate([source[rows_away:], padding], axis=0)
    return (earlier, later)


def shards(
    sequence_in,
    output_grad,
    skip_mask,
    in_gain,
    input_shift_vec,
    mid_gain,
    mid_offset,
    conv_weight,
    point_weight,
):
    peers = lax.axis_size("seq")
    channels = sequence_in.shape[2]
    block_shape = conv_weight.shape[1:]
    conv_rows = conv_weight[0].size // channels
    first_weights = jnp.concatenate(
        [conv_weight[0].reshape(-1, channels), point_weight.reshape(-1, channels)]
    )
    state_pieces, first_halves = exchanged(
        [
            strided_pieces(sequence_in[0], peers),
            half_for_each(first_weights, peers, channels),
        ],
        "seq",
    )
    state = state_pieces.reshape(-1, channels)
    grad_rows_sent = strided_pieces(output_grad[0], peers)
    second_joined = jnp.concatenate(
        [grad_rows_sent, half_for_each(conv_weight[1], peers, channels)], axis=1
    )
    second_joined, state = lax.optimization_barrier((second_joined, state))
    second_arrived = lax.all_to_all(second_joined, "seq", 0, 0, tiled=True)
    grad_pieces = second_arrived[:, : grad_rows_sent.shape[1]]
    second_halves = second_arrived[:, grad_rows_sent.shape[1] :]
    first_whole = whole_from_halves(first_halves, "seq")
    first_pieces = first_whole[:, :conv_rows]
    point_full = first_whole[:, conv_rows:].reshape(-1, *point_weight.shape[1:])
    second_pieces = whole_from_halves(second_halves, "seq")
    conv_full = [
        conv_from_pieces(first_pieces, block_shape),
        conv_from_pieces(second_pieces, block_shape),
    ]
    row_reach = (FIRST_DILATION // peers, SECOND_DILATION // peers)
    saved = []
    for block_index in range(2):
        kept_flag = (1 - skip_mask[0, block_index]).astype(jnp.float32)
        normed = state.astype(jnp.float32) * in_gain[block_index] + input_shift_vec[block_index]
        activated = gelu_tanh(normed).astype(jnp.bfloat16)
        earlier, later = row_shifted(activated, row_reach[block_index])
        operands = (
            state,
            earlier,
            activated,
            later,
            conv_full[block_index],
            mid_gain[block_index],
            mid_offset[block_index],
            point_full[:, block_index, :],
            kept_flag,
        )
        middle, hidden_act, state = forward_local(*operands)
        saved.append((normed, middle, hidden_act, kept_flag))
    gradient = grad_pieces.reshape(-1, channels)
    terms = [None, None]
    for block_index in (1, 0):
        normed, middle, hidden_act, kept_flag = saved[block_index]
        projection = point_full[:, block_index, :]
        first_operands = (gradient, middle, projection, mid_gain[block_index], kept_flag)
        conv_grad, branch_grad = backward_first(*first_operands)
        terms[block_index] = chip_half(grad_rows(hidden_act, branch_grad), peers, channels)
        earlier, later = row_shifted(conv_grad, row_reach[block_index])
        second_operands = (
            gradient,
            earlier,
            conv_grad,
            later,
            conv_full[block_index],
            normed,
            in_gain[block_index],
        )
        gradient = backward_second(*second_operands)
        if block_index == 1:
            terms[1], gradient = lax.optimization_barrier((terms[1], gradient))
    first_term, second_term, back_pieces = exchanged(
        terms + [gradient.reshape(peers, -1, channels)], "seq"
    )
    own_terms = [chip_sum(piece, peers, channels) for piece in (first_term, second_term)]
    summed = reduced_over_dp(jnp.stack(own_terms, axis=1))
    sample_count = sequence_in.shape[0] * lax.axis_size("dp")
    full_length = sequence_in.shape[1] * peers
    point_grad = summed * (1.0 / math.sqrt(sample_count * full_length))
    input_grad = back_pieces.reshape(sequence_in.shape)
    return (point_grad, input_grad)


def solution(mesh):
    return jax.shard_map(
        shards,
        mesh=mesh,
        in_specs=(
            P("dp", "seq", None),
            P("dp", "seq", None),
            P("dp", None),
            P(),
            P(),
            P(),
            P(),
            P(None, None, "seq", None),
            P("seq", None, None),
        ),
        out_specs=(P("seq", None, None), P("dp", "seq", None)),
        check_vma=False,
    )
```

```python
import math

import jax
import jax.numpy as jnp
from jax import lax
from jax.sharding import PartitionSpec as P

FIRST_DILATION = 1024
SECOND_DILATION = 2048


def passed_along(value, axis, by):
    peers = lax.axis_size(axis)
    pairs = [(i, i + by) for i in range(peers) if 0 <= i + by < peers]
    return lax.ppermute(value, axis, pairs)


def gathered(value, axis):
    peers = lax.axis_size(axis)
    copies = jnp.broadcast_to(value[None], (peers,) + value.shape)
    return lax.all_to_all(copies, axis, 0, 0, tiled=True)


def summed_over(value, axis, sent_as=jnp.float32):
    peers = lax.axis_size(axis)
    pieces = value.reshape((peers, -1) + value.shape[1:]).astype(sent_as)
    arrived = lax.all_to_all(pieces, axis, 0, 0, tiled=True)
    return arrived.astype(jnp.float32).sum(axis=0)


def reduced_over_dp(value):
    dp_size = lax.axis_size("dp")
    own_piece = summed_over(value.reshape(dp_size, -1), "dp", jnp.bfloat16)
    return gathered(own_piece, "dp").reshape(value.shape)


def gelu_tanh(values):
    return jax.nn.gelu(values, approximate=True)


def contract_last(left, right):
    return lax.dot_general(
        left, right, (((1,), (1,)), ((), ())), preferred_element_type=jnp.float32
    )


def neighbours(source, shards_away):
    earlier = passed_along(source, "seq", shards_away)
    later = passed_along(source, "seq", -shards_away)
    return (earlier, later)


def forward_local(
    state, earlier, activated, later, weight, gain_vec, offset_vec, projection, kept_flag
):
    conv_out = jnp.dot(earlier, weight[0], preferred_element_type=jnp.float32)
    conv_out = conv_out + jnp.dot(activated, weight[1], preferred_element_type=jnp.float32)
    conv_out = conv_out + jnp.dot(later, weight[2], preferred_element_type=jnp.float32)
    middle = conv_out * gain_vec + offset_vec
    hidden_act = gelu_tanh(middle).astype(jnp.bfloat16)
    branch = jnp.dot(hidden_act, projection, preferred_element_type=jnp.float32)
    result = (state.astype(jnp.float32) + kept_flag * branch).astype(jnp.bfloat16)
    return (middle, hidden_act, result)


def backward_first(gradient, middle, projection, gain_vec, kept_flag):
    branch_grad = (kept_flag * gradient.astype(jnp.float32)).astype(jnp.bfloat16)
    hidden_grad = contract_last(branch_grad, projection)
    middle_grad = jax.vjp(gelu_tanh, middle)[1](hidden_grad)[0]
    conv_grad = (middle_grad * gain_vec).astype(jnp.bfloat16)
    return (conv_grad, branch_grad)


def backward_second(gradient, earlier, conv_grad, later, weight, normed, gain_vec):
    act_grad = (
        contract_last(later, weight[0])
        + contract_last(conv_grad, weight[1])
        + contract_last(earlier, weight[2])
    )
    normed_grad = jax.vjp(gelu_tanh, normed)[1](act_grad)[0] * gain_vec
    return (gradient.astype(jnp.float32) + normed_grad).astype(jnp.bfloat16)


def grad_rows(hidden_act, branch_grad):
    return lax.dot_general(
        hidden_act, branch_grad, (((0,), (0,)), ((), ())), preferred_element_type=jnp.float32
    )


def exchanged(parts, axis):
    joined = jnp.concatenate(parts, axis=1)
    arrived = lax.all_to_all(joined, axis, 0, 0, tiled=True)
    pieces = []
    offset = 0
    for part in parts:
        pieces.append(arrived[:, offset : offset + part.shape[1]])
        offset += part.shape[1]
    return pieces


def strided_pieces(block, peers):
    return block.reshape(peers, -1, block.shape[-1])


def half_for_each(shard, peers, lanes):
    halves = shard.reshape(2, -1, lanes)
    return jnp.tile(halves, (peers // 2, 1, 1))


def whole_from_halves(own_halves, axis):
    peers = lax.axis_size(axis)
    partner = lax.ppermute(own_halves, axis, [(i, i ^ 1) for i in range(peers)])
    first_core = lax.axis_index(axis) % 2 == 0
    low = jnp.where(first_core, own_halves, partner)
    high = jnp.where(first_core, partner, own_halves)
    return jnp.concatenate([low, high], axis=1)


def conv_from_pieces(pieces, block_shape):
    taps, rows, hidden = block_shape
    parts = pieces.reshape(-1, taps, rows, hidden)
    return jnp.moveaxis(parts, 0, 1).reshape(taps, -1, hidden)


def chip_half(term, peers, channels):
    half = channels // 2
    first_core = lax.axis_index("seq") % 2 == 0
    kept = jnp.where(first_core, term[:, :half], term[:, half:])
    given = jnp.where(first_core, term[:, half:], term[:, :half])
    partner = lax.ppermute(given, "seq", [(i, i ^ 1) for i in range(peers)])
    summed = (kept + partner).astype(jnp.bfloat16)
    return summed.reshape(peers, -1, channels)


def chip_sum(piece, peers, channels):
    half = channels // 2
    parts = piece.reshape(peers // 2, 2, -1, half).astype(jnp.float32).sum(axis=0)
    return jnp.moveaxis(parts, 0, 1).reshape(-1, channels)


def row_shifted(source, rows_away):
    padding = jnp.zeros((rows_away, source.shape[1]), source.dtype)
    earlier = jnp.concatenate([padding, source[: source.shape[0] - rows_away]], axis=0)
    later = jnp.concatenate([source[rows_away:], padding], axis=0)
    return (earlier, later)


def shards(
    sequence_in,
    output_grad,
    skip_mask,
    in_gain,
    input_shift_vec,
    mid_gain,
    mid_offset,
    conv_weight,
    point_weight,
):
    peers = lax.axis_size("seq")
    channels = sequence_in.shape[2]
    block_shape = conv_weight.shape[1:]
    conv_rows = conv_weight[0].size // channels
    first_weights = jnp.concatenate(
        [conv_weight[0].reshape(-1, channels), point_weight[:, 0, :]]
    )
    state_pieces, first_halves = exchanged(
        [
            strided_pieces(sequence_in[0], peers),
            half_for_each(first_weights, peers, channels),
        ],
        "seq",
    )
    state = state_pieces.reshape(-1, channels)
    grad_rows_sent = strided_pieces(output_grad[0], peers)
    second_weights = jnp.concatenate(
        [conv_weight[1].reshape(-1, channels), point_weight[:, 1, :]]
    )
    second_joined = jnp.concatenate(
        [grad_rows_sent, half_for_each(second_weights, peers, channels)], axis=1
    )
    second_joined, state = lax.optimization_barrier((second_joined, state))
    second_arrived = lax.all_to_all(second_joined, "seq", 0, 0, tiled=True)
    grad_pieces = second_arrived[:, : grad_rows_sent.shape[1]]
    second_halves = second_arrived[:, grad_rows_sent.shape[1] :]
    wholes = [whole_from_halves(first_halves, "seq"), whole_from_halves(second_halves, "seq")]
    conv_full = [conv_from_pieces(whole[:, :conv_rows], block_shape) for whole in wholes]
    point_blocks = [whole[:, conv_rows:].reshape(-1, channels) for whole in wholes]
    row_reach = (FIRST_DILATION // peers, SECOND_DILATION // peers)
    saved = []
    for block_index in range(2):
        kept_flag = (1 - skip_mask[0, block_index]).astype(jnp.float32)
        normed = state.astype(jnp.float32) * in_gain[block_index] + input_shift_vec[block_index]
        activated = gelu_tanh(normed).astype(jnp.bfloat16)
        earlier, later = row_shifted(activated, row_reach[block_index])
        operands = (
            state,
            earlier,
            activated,
            later,
            conv_full[block_index],
            mid_gain[block_index],
            mid_offset[block_index],
            point_blocks[block_index],
            kept_flag,
        )
        middle, hidden_act, state = forward_local(*operands)
        saved.append((normed, middle, hidden_act, kept_flag))
    gradient = grad_pieces.reshape(-1, channels)
    terms = [None, None]
    for block_index in (1, 0):
        normed, middle, hidden_act, kept_flag = saved[block_index]
        projection = point_blocks[block_index]
        first_operands = (gradient, middle, projection, mid_gain[block_index], kept_flag)
        conv_grad, branch_grad = backward_first(*first_operands)
        terms[block_index] = chip_half(grad_rows(hidden_act, branch_grad), peers, channels)
        earlier, later = row_shifted(conv_grad, row_reach[block_index])
        second_operands = (
            gradient,
            earlier,
            conv_grad,
            later,
            conv_full[block_index],
            normed,
            in_gain[block_index],
        )
        gradient = backward_second(*second_operands)
        if block_index == 1:
            terms[1], gradient = lax.optimization_barrier((terms[1], gradient))
    first_term, second_term, back_pieces = exchanged(
        terms + [gradient.reshape(peers, -1, channels)], "seq"
    )
    own_terms = [chip_sum(piece, peers, channels) for piece in (first_term, second_term)]
    summed = reduced_over_dp(jnp.stack(own_terms, axis=1))
    sample_count = sequence_in.shape[0] * lax.axis_size("dp")
    full_length = sequence_in.shape[1] * peers
    point_grad = summed * (1.0 / math.sqrt(sample_count * full_length))
    input_grad = back_pieces.reshape(sequence_in.shape)
    return (point_grad, input_grad)


def solution(mesh):
    return jax.shard_map(
        shards,
        mesh=mesh,
        in_specs=(
            P("dp", "seq", None),
            P("dp", "seq", None),
            P("dp", None),
            P(),
            P(),
            P(),
            P(),
            P(None, None, "seq", None),
            P("seq", None, None),
        ),
        out_specs=(P("seq", None, None), P("dp", "seq", None)),
        check_vma=False,
    )
```

```python
import math

import jax
import jax.numpy as jnp
from jax import lax
from jax.sharding import PartitionSpec as P

FIRST_DILATION = 1024
SECOND_DILATION = 2048


def passed_along(value, axis, by):
    peers = lax.axis_size(axis)
    pairs = [(i, i + by) for i in range(peers) if 0 <= i + by < peers]
    return lax.ppermute(value, axis, pairs)


def gathered(value, axis):
    peers = lax.axis_size(axis)
    copies = jnp.broadcast_to(value[None], (peers,) + value.shape)
    return lax.all_to_all(copies, axis, 0, 0, tiled=True)


def summed_over(value, axis, sent_as=jnp.float32):
    peers = lax.axis_size(axis)
    pieces = value.reshape((peers, -1) + value.shape[1:]).astype(sent_as)
    arrived = lax.all_to_all(pieces, axis, 0, 0, tiled=True)
    return arrived.astype(jnp.float32).sum(axis=0)


def reduced_over_dp(value):
    dp_size = lax.axis_size("dp")
    own_piece = summed_over(value.reshape(dp_size, -1), "dp", jnp.bfloat16)
    return gathered(own_piece, "dp").reshape(value.shape)


def gelu_tanh(values):
    return jax.nn.gelu(values, approximate=True)


def contract_last(left, right):
    return lax.dot_general(
        left, right, (((1,), (1,)), ((), ())), preferred_element_type=jnp.float32
    )


def neighbours(source, shards_away):
    earlier = passed_along(source, "seq", shards_away)
    later = passed_along(source, "seq", -shards_away)
    return (earlier, later)


def forward_local(
    state, earlier, activated, later, weight, gain_vec, offset_vec, projection, kept_flag
):
    conv_out = jnp.dot(earlier, weight[0], preferred_element_type=jnp.float32)
    conv_out = conv_out + jnp.dot(activated, weight[1], preferred_element_type=jnp.float32)
    conv_out = conv_out + jnp.dot(later, weight[2], preferred_element_type=jnp.float32)
    middle = conv_out * gain_vec + offset_vec
    hidden_act = gelu_tanh(middle).astype(jnp.bfloat16)
    branch = jnp.dot(hidden_act, projection, preferred_element_type=jnp.float32)
    result = (state.astype(jnp.float32) + kept_flag * branch).astype(jnp.bfloat16)
    return (middle, hidden_act, result)


def backward_first(gradient, middle, projection, gain_vec, kept_flag):
    branch_grad = (kept_flag * gradient.astype(jnp.float32)).astype(jnp.bfloat16)
    hidden_grad = contract_last(branch_grad, projection)
    middle_grad = jax.vjp(gelu_tanh, middle)[1](hidden_grad)[0]
    conv_grad = (middle_grad * gain_vec).astype(jnp.bfloat16)
    return (conv_grad, branch_grad)


def backward_second(gradient, earlier, conv_grad, later, weight, normed, gain_vec):
    act_grad = (
        contract_last(later, weight[0])
        + contract_last(conv_grad, weight[1])
        + contract_last(earlier, weight[2])
    )
    normed_grad = jax.vjp(gelu_tanh, normed)[1](act_grad)[0] * gain_vec
    return (gradient.astype(jnp.float32) + normed_grad).astype(jnp.bfloat16)


def grad_rows(hidden_act, branch_grad):
    return lax.dot_general(
        hidden_act, branch_grad, (((0,), (0,)), ((), ())), preferred_element_type=jnp.float32
    )


def exchanged(parts, axis):
    joined = jnp.concatenate(parts, axis=1)
    arrived = lax.all_to_all(joined, axis, 0, 0, tiled=True)
    pieces = []
    offset = 0
    for part in parts:
        pieces.append(arrived[:, offset : offset + part.shape[1]])
        offset += part.shape[1]
    return pieces


def strided_pieces(block, peers):
    return block.reshape(peers, -1, block.shape[-1])


def half_for_each(shard, peers, lanes):
    halves = shard.reshape(2, -1, lanes)
    return jnp.tile(halves, (peers // 2, 1, 1))


def whole_from_halves(own_halves, axis):
    peers = lax.axis_size(axis)
    partner = lax.ppermute(own_halves, axis, [(i, i ^ 1) for i in range(peers)])
    first_core = lax.axis_index(axis) % 2 == 0
    low = jnp.where(first_core, own_halves, partner)
    high = jnp.where(first_core, partner, own_halves)
    return jnp.concatenate([low, high], axis=1)


def conv_from_pieces(pieces, block_shape):
    taps, rows, hidden = block_shape
    parts = pieces.reshape(-1, taps, rows, hidden)
    return jnp.moveaxis(parts, 0, 1).reshape(taps, -1, hidden)


def chip_half(term, peers, channels):
    half = channels // 2
    first_core = lax.axis_index("seq") % 2 == 0
    kept = jnp.where(first_core, term[:, :half], term[:, half:])
    given = jnp.where(first_core, term[:, half:], term[:, :half])
    partner = lax.ppermute(given, "seq", [(i, i ^ 1) for i in range(peers)])
    summed = (kept + partner).astype(jnp.bfloat16)
    return summed.reshape(peers, -1, channels)


def chip_sum(piece, peers, channels):
    half = channels // 2
    parts = piece.reshape(peers // 2, 2, -1, half).astype(jnp.float32).sum(axis=0)
    return jnp.moveaxis(parts, 0, 1).reshape(-1, channels)


def row_shifted(source, rows_away):
    padding = jnp.zeros((rows_away, source.shape[1]), source.dtype)
    earlier = jnp.concatenate([padding, source[: source.shape[0] - rows_away]], axis=0)
    later = jnp.concatenate([source[rows_away:], padding], axis=0)
    return (earlier, later)


def shards(
    sequence_in,
    output_grad,
    skip_mask,
    in_gain,
    input_shift_vec,
    mid_gain,
    mid_offset,
    conv_weight,
    point_weight,
):
    peers = lax.axis_size("seq")
    channels = sequence_in.shape[2]
    block_shape = conv_weight.shape[1:]
    conv_rows = conv_weight[0].size // channels
    first_weights = jnp.concatenate(
        [conv_weight[0].reshape(-1, channels), point_weight[:, 0, :]]
    )
    state_pieces, first_halves = exchanged(
        [
            strided_pieces(sequence_in[0], peers),
            half_for_each(first_weights, peers, channels),
        ],
        "seq",
    )
    state = state_pieces.reshape(-1, channels)
    grad_rows_sent = strided_pieces(output_grad[0], peers)
    second_weights = jnp.concatenate(
        [conv_weight[1].reshape(-1, channels), point_weight[:, 1, :]]
    )
    second_joined = jnp.concatenate(
        [grad_rows_sent, half_for_each(second_weights, peers, channels)], axis=1
    )
    second_joined, state = lax.optimization_barrier((second_joined, state))
    second_arrived = lax.all_to_all(second_joined, "seq", 0, 0, tiled=True)
    grad_pieces = second_arrived[:, : grad_rows_sent.shape[1]]
    second_halves = second_arrived[:, grad_rows_sent.shape[1] :]
    wholes = [whole_from_halves(first_halves, "seq"), whole_from_halves(second_halves, "seq")]
    conv_full = [conv_from_pieces(whole[:, :conv_rows], block_shape) for whole in wholes]
    point_blocks = [whole[:, conv_rows:].reshape(-1, channels) for whole in wholes]
    row_reach = (FIRST_DILATION // peers, SECOND_DILATION // peers)
    saved = []
    for block_index in range(2):
        kept_flag = (1 - skip_mask[0, block_index]).astype(jnp.float32)
        normed = state.astype(jnp.float32) * in_gain[block_index] + input_shift_vec[block_index]
        activated = gelu_tanh(normed).astype(jnp.bfloat16)
        earlier, later = row_shifted(activated, row_reach[block_index])
        operands = (
            state,
            earlier,
            activated,
            later,
            conv_full[block_index],
            mid_gain[block_index],
            mid_offset[block_index],
            point_blocks[block_index],
            kept_flag,
        )
        middle, hidden_act, state = forward_local(*operands)
        saved.append((normed, middle, hidden_act, kept_flag))
    gradient = grad_pieces.reshape(-1, channels)
    terms = [None, None]
    for block_index in (1, 0):
        normed, middle, hidden_act, kept_flag = saved[block_index]
        projection = point_blocks[block_index]
        first_operands = (gradient, middle, projection, mid_gain[block_index], kept_flag)
        conv_grad, branch_grad = backward_first(*first_operands)
        term = grad_rows(hidden_act, branch_grad)
        if block_index == 1:
            terms[1] = chip_half(term, peers, channels)
        else:
            terms[0] = term.astype(jnp.bfloat16).reshape(peers, -1, channels)
        earlier, later = row_shifted(conv_grad, row_reach[block_index])
        second_operands = (
            gradient,
            earlier,
            conv_grad,
            later,
            conv_full[block_index],
            normed,
            in_gain[block_index],
        )
        gradient = backward_second(*second_operands)
        if block_index == 1:
            terms[1], gradient = lax.optimization_barrier((terms[1], gradient))
    first_term, second_term, back_pieces = exchanged(
        terms + [gradient.reshape(peers, -1, channels)], "seq"
    )
    own_terms = [first_term.astype(jnp.float32).sum(axis=0), chip_sum(second_term, peers, channels)]
    summed = reduced_over_dp(jnp.stack(own_terms, axis=1))
    sample_count = sequence_in.shape[0] * lax.axis_size("dp")
    full_length = sequence_in.shape[1] * peers
    point_grad = summed * (1.0 / math.sqrt(sample_count * full_length))
    input_grad = back_pieces.reshape(sequence_in.shape)
    return (point_grad, input_grad)


def solution(mesh):
    return jax.shard_map(
        shards,
        mesh=mesh,
        in_specs=(
            P("dp", "seq", None),
            P("dp", "seq", None),
            P("dp", None),
            P(),
            P(),
            P(),
            P(),
            P(None, None, "seq", None),
            P("seq", None, None),
        ),
        out_specs=(P("seq", None, None), P("dp", "seq", None)),
        check_vma=False,
    )
```

```python
import math

import jax
import jax.numpy as jnp
from jax import lax
from jax.sharding import PartitionSpec as P

FIRST_DILATION = 1024
SECOND_DILATION = 2048


def passed_along(value, axis, by):
    peers = lax.axis_size(axis)
    pairs = [(i, i + by) for i in range(peers) if 0 <= i + by < peers]
    return lax.ppermute(value, axis, pairs)


def gathered(value, axis):
    peers = lax.axis_size(axis)
    copies = jnp.broadcast_to(value[None], (peers,) + value.shape)
    return lax.all_to_all(copies, axis, 0, 0, tiled=True)


def summed_over(value, axis, sent_as=jnp.float32):
    peers = lax.axis_size(axis)
    pieces = value.reshape((peers, -1) + value.shape[1:]).astype(sent_as)
    arrived = lax.all_to_all(pieces, axis, 0, 0, tiled=True)
    return arrived.astype(jnp.float32).sum(axis=0)


def reduced_over_dp(value):
    dp_size = lax.axis_size("dp")
    own_piece = summed_over(value.reshape(dp_size, -1), "dp", jnp.bfloat16)
    return gathered(own_piece, "dp").reshape(value.shape)


def gelu_tanh(values):
    return jax.nn.gelu(values, approximate=True)


def contract_last(left, right):
    return lax.dot_general(
        left, right, (((1,), (1,)), ((), ())), preferred_element_type=jnp.float32
    )


def neighbours(source, shards_away):
    earlier = passed_along(source, "seq", shards_away)
    later = passed_along(source, "seq", -shards_away)
    return (earlier, later)


def forward_local(
    state, earlier, activated, later, weight, gain_vec, offset_vec, projection, kept_flag
):
    conv_out = jnp.dot(earlier, weight[0], preferred_element_type=jnp.float32)
    conv_out = conv_out + jnp.dot(activated, weight[1], preferred_element_type=jnp.float32)
    conv_out = conv_out + jnp.dot(later, weight[2], preferred_element_type=jnp.float32)
    middle = conv_out * gain_vec + offset_vec
    hidden_act = gelu_tanh(middle).astype(jnp.bfloat16)
    branch = jnp.dot(hidden_act, projection, preferred_element_type=jnp.float32)
    result = (state.astype(jnp.float32) + kept_flag * branch).astype(jnp.bfloat16)
    return (middle, hidden_act, result)


def backward_first(gradient, middle, projection, gain_vec, kept_flag):
    branch_grad = (kept_flag * gradient.astype(jnp.float32)).astype(jnp.bfloat16)
    hidden_grad = contract_last(branch_grad, projection)
    middle_grad = jax.vjp(gelu_tanh, middle)[1](hidden_grad)[0]
    conv_grad = (middle_grad * gain_vec).astype(jnp.bfloat16)
    return (conv_grad, branch_grad)


def backward_second(gradient, earlier, conv_grad, later, weight, normed, gain_vec):
    act_grad = (
        contract_last(later, weight[0])
        + contract_last(conv_grad, weight[1])
        + contract_last(earlier, weight[2])
    )
    normed_grad = jax.vjp(gelu_tanh, normed)[1](act_grad)[0] * gain_vec
    return (gradient.astype(jnp.float32) + normed_grad).astype(jnp.bfloat16)


def grad_rows(hidden_act, branch_grad):
    return lax.dot_general(
        hidden_act, branch_grad, (((0,), (0,)), ((), ())), preferred_element_type=jnp.float32
    )


def exchanged(parts, axis):
    joined = jnp.concatenate(parts, axis=1)
    arrived = lax.all_to_all(joined, axis, 0, 0, tiled=True)
    pieces = []
    offset = 0
    for part in parts:
        pieces.append(arrived[:, offset : offset + part.shape[1]])
        offset += part.shape[1]
    return pieces


def strided_pieces(block, peers):
    return block.reshape(peers, -1, block.shape[-1])


def half_for_each(shard, peers, lanes):
    halves = shard.reshape(2, -1, lanes)
    return jnp.tile(halves, (peers // 2, 1, 1))


def whole_from_halves(own_halves, axis):
    peers = lax.axis_size(axis)
    partner = lax.ppermute(own_halves, axis, [(i, i ^ 1) for i in range(peers)])
    first_core = lax.axis_index(axis) % 2 == 0
    low = jnp.where(first_core, own_halves, partner)
    high = jnp.where(first_core, partner, own_halves)
    return jnp.concatenate([low, high], axis=1)


def conv_from_pieces(pieces, block_shape):
    taps, rows, hidden = block_shape
    parts = pieces.reshape(-1, taps, rows, hidden)
    return jnp.moveaxis(parts, 0, 1).reshape(taps, -1, hidden)


def chip_half(term, peers, channels):
    half = channels // 2
    first_core = lax.axis_index("seq") % 2 == 0
    kept = jnp.where(first_core, term[:, :half], term[:, half:])
    given = jnp.where(first_core, term[:, half:], term[:, :half])
    partner = lax.ppermute(given, "seq", [(i, i ^ 1) for i in range(peers)])
    summed = (kept + partner).astype(jnp.bfloat16)
    return summed.reshape(peers, -1, channels)


def chip_sum(piece, peers, channels):
    half = channels // 2
    parts = piece.reshape(peers // 2, 2, -1, half).astype(jnp.float32).sum(axis=0)
    return jnp.moveaxis(parts, 0, 1).reshape(-1, channels)


def row_shifted(source, rows_away):
    padding = jnp.zeros((rows_away, source.shape[1]), source.dtype)
    earlier = jnp.concatenate([padding, source[: source.shape[0] - rows_away]], axis=0)
    later = jnp.concatenate([source[rows_away:], padding], axis=0)
    return (earlier, later)


def shards(
    sequence_in,
    output_grad,
    skip_mask,
    in_gain,
    input_shift_vec,
    mid_gain,
    mid_offset,
    conv_weight,
    point_weight,
):
    peers = lax.axis_size("seq")
    channels = sequence_in.shape[2]
    block_shape = conv_weight.shape[1:]
    conv_rows = conv_weight[0].size // channels
    first_weights = jnp.concatenate(
        [conv_weight[0].reshape(-1, channels), point_weight[:, 0, :]]
    )
    state_pieces, first_halves = exchanged(
        [
            strided_pieces(sequence_in[0], peers),
            half_for_each(first_weights, peers, channels),
        ],
        "seq",
    )
    state = state_pieces.reshape(-1, channels)
    grad_rows_sent = strided_pieces(output_grad[0], peers)
    second_weights = jnp.concatenate(
        [conv_weight[1].reshape(-1, channels), point_weight[:, 1, :]]
    )
    second_joined = jnp.concatenate(
        [grad_rows_sent, half_for_each(second_weights, peers, channels)], axis=1
    )
    second_arrived = lax.all_to_all(second_joined, "seq", 0, 0, tiled=True)
    grad_pieces = second_arrived[:, : grad_rows_sent.shape[1]]
    second_halves = second_arrived[:, grad_rows_sent.shape[1] :]
    wholes = [whole_from_halves(first_halves, "seq"), whole_from_halves(second_halves, "seq")]
    conv_full = [conv_from_pieces(whole[:, :conv_rows], block_shape) for whole in wholes]
    point_blocks = [whole[:, conv_rows:].reshape(-1, channels) for whole in wholes]
    row_reach = (FIRST_DILATION // peers, SECOND_DILATION // peers)
    saved = []
    for block_index in range(2):
        kept_flag = (1 - skip_mask[0, block_index]).astype(jnp.float32)
        normed = state.astype(jnp.float32) * in_gain[block_index] + input_shift_vec[block_index]
        activated = gelu_tanh(normed).astype(jnp.bfloat16)
        earlier, later = row_shifted(activated, row_reach[block_index])
        operands = (
            state,
            earlier,
            activated,
            later,
            conv_full[block_index],
            mid_gain[block_index],
            mid_offset[block_index],
            point_blocks[block_index],
            kept_flag,
        )
        middle, hidden_act, state = forward_local(*operands)
        saved.append((normed, middle, hidden_act, kept_flag))
    gradient = grad_pieces.reshape(-1, channels)
    terms = [None, None]
    for block_index in (1, 0):
        normed, middle, hidden_act, kept_flag = saved[block_index]
        projection = point_blocks[block_index]
        first_operands = (gradient, middle, projection, mid_gain[block_index], kept_flag)
        conv_grad, branch_grad = backward_first(*first_operands)
        terms[block_index] = chip_half(grad_rows(hidden_act, branch_grad), peers, channels)
        earlier, later = row_shifted(conv_grad, row_reach[block_index])
        second_operands = (
            gradient,
            earlier,
            conv_grad,
            later,
            conv_full[block_index],
            normed,
            in_gain[block_index],
        )
        gradient = backward_second(*second_operands)
        if block_index == 1:
            terms[1], gradient = lax.optimization_barrier((terms[1], gradient))
    first_term, second_term, back_pieces = exchanged(
        terms + [gradient.reshape(peers, -1, channels)], "seq"
    )
    own_terms = [chip_sum(piece, peers, channels) for piece in (first_term, second_term)]
    summed = reduced_over_dp(jnp.stack(own_terms, axis=1))
    sample_count = sequence_in.shape[0] * lax.axis_size("dp")
    full_length = sequence_in.shape[1] * peers
    point_grad = summed * (1.0 / math.sqrt(sample_count * full_length))
    input_grad = back_pieces.reshape(sequence_in.shape)
    return (point_grad, input_grad)


def solution(mesh):
    return jax.shard_map(
        shards,
        mesh=mesh,
        in_specs=(
            P("dp", "seq", None),
            P("dp", "seq", None),
            P("dp", None),
            P(),
            P(),
            P(),
            P(),
            P(None, None, "seq", None),
            P("seq", None, None),
        ),
        out_specs=(P("seq", None, None), P("dp", "seq", None)),
        check_vma=False,
    )
```

```python
import math

import jax
import jax.numpy as jnp
from jax import lax
from jax.sharding import PartitionSpec as P

FIRST_DILATION = 1024
SECOND_DILATION = 2048


def passed_along(value, axis, by):
    peers = lax.axis_size(axis)
    pairs = [(i, i + by) for i in range(peers) if 0 <= i + by < peers]
    return lax.ppermute(value, axis, pairs)


def gathered(value, axis):
    peers = lax.axis_size(axis)
    copies = jnp.broadcast_to(value[None], (peers,) + value.shape)
    return lax.all_to_all(copies, axis, 0, 0, tiled=True)


def summed_over(value, axis, sent_as=jnp.float32):
    peers = lax.axis_size(axis)
    pieces = value.reshape((peers, -1) + value.shape[1:]).astype(sent_as)
    arrived = lax.all_to_all(pieces, axis, 0, 0, tiled=True)
    return arrived.astype(jnp.float32).sum(axis=0)


def reduced_over_dp(value):
    dp_size = lax.axis_size("dp")
    own_piece = summed_over(value.reshape(dp_size, -1), "dp", jnp.bfloat16)
    return gathered(own_piece, "dp").reshape(value.shape)


def gelu_tanh(values):
    return jax.nn.gelu(values, approximate=True)


def contract_last(left, right):
    return lax.dot_general(
        left, right, (((1,), (1,)), ((), ())), preferred_element_type=jnp.float32
    )


def neighbours(source, shards_away):
    earlier = passed_along(source, "seq", shards_away)
    later = passed_along(source, "seq", -shards_away)
    return (earlier, later)


def forward_local(
    state, earlier, activated, later, weight, gain_vec, offset_vec, projection, kept_flag
):
    conv_out = jnp.dot(earlier, weight[0], preferred_element_type=jnp.float32)
    conv_out = conv_out + jnp.dot(activated, weight[1], preferred_element_type=jnp.float32)
    conv_out = conv_out + jnp.dot(later, weight[2], preferred_element_type=jnp.float32)
    middle = conv_out * gain_vec + offset_vec
    hidden_act = gelu_tanh(middle).astype(jnp.bfloat16)
    branch = jnp.dot(hidden_act, projection, preferred_element_type=jnp.float32)
    result = (state.astype(jnp.float32) + kept_flag * branch).astype(jnp.bfloat16)
    return (middle, hidden_act, result)


def backward_first(gradient, middle, projection, gain_vec, kept_flag):
    branch_grad = (kept_flag * gradient.astype(jnp.float32)).astype(jnp.bfloat16)
    hidden_grad = contract_last(branch_grad, projection)
    middle_grad = jax.vjp(gelu_tanh, middle)[1](hidden_grad)[0]
    conv_grad = (middle_grad * gain_vec).astype(jnp.bfloat16)
    return (conv_grad, branch_grad)


def backward_second(gradient, earlier, conv_grad, later, weight, normed, gain_vec):
    act_grad = (
        contract_last(later, weight[0])
        + contract_last(conv_grad, weight[1])
        + contract_last(earlier, weight[2])
    )
    normed_grad = jax.vjp(gelu_tanh, normed)[1](act_grad)[0] * gain_vec
    return (gradient.astype(jnp.float32) + normed_grad).astype(jnp.bfloat16)


def grad_rows(hidden_act, branch_grad):
    return lax.dot_general(
        hidden_act, branch_grad, (((0,), (0,)), ((), ())), preferred_element_type=jnp.float32
    )


def exchanged(parts, axis):
    joined = jnp.concatenate(parts, axis=1)
    arrived = lax.all_to_all(joined, axis, 0, 0, tiled=True)
    pieces = []
    offset = 0
    for part in parts:
        pieces.append(arrived[:, offset : offset + part.shape[1]])
        offset += part.shape[1]
    return pieces


def strided_pieces(block, peers):
    return block.reshape(peers, -1, block.shape[-1])


def half_for_each(shard, peers, lanes):
    halves = shard.reshape(2, -1, lanes)
    return jnp.tile(halves, (peers // 2, 1, 1))


def whole_from_halves(own_halves, axis):
    peers = lax.axis_size(axis)
    partner = lax.ppermute(own_halves, axis, [(i, i ^ 1) for i in range(peers)])
    first_core = lax.axis_index(axis) % 2 == 0
    low = jnp.where(first_core, own_halves, partner)
    high = jnp.where(first_core, partner, own_halves)
    return jnp.concatenate([low, high], axis=1)


def conv_from_pieces(pieces, block_shape):
    taps, rows, hidden = block_shape
    parts = pieces.reshape(-1, taps, rows, hidden)
    return jnp.moveaxis(parts, 0, 1).reshape(taps, -1, hidden)


def chip_half(term, peers, channels):
    half = channels // 2
    first_core = lax.axis_index("seq") % 2 == 0
    kept = jnp.where(first_core, term[:, :half], term[:, half:])
    given = jnp.where(first_core, term[:, half:], term[:, :half])
    partner = lax.ppermute(given, "seq", [(i, i ^ 1) for i in range(peers)])
    summed = (kept + partner).astype(jnp.bfloat16)
    return summed.reshape(peers, -1, channels)


def chip_sum(piece, peers, channels):
    half = channels // 2
    parts = piece.reshape(peers // 2, 2, -1, half).astype(jnp.float32).sum(axis=0)
    return jnp.moveaxis(parts, 0, 1).reshape(-1, channels)


def row_shifted(source, rows_away):
    padding = jnp.zeros((rows_away, source.shape[1]), source.dtype)
    earlier = jnp.concatenate([padding, source[: source.shape[0] - rows_away]], axis=0)
    later = jnp.concatenate([source[rows_away:], padding], axis=0)
    return (earlier, later)


def shards(
    sequence_in,
    output_grad,
    skip_mask,
    in_gain,
    input_shift_vec,
    mid_gain,
    mid_offset,
    conv_weight,
    point_weight,
):
    peers = lax.axis_size("seq")
    channels = sequence_in.shape[2]
    block_shape = conv_weight.shape[1:]
    conv_rows = conv_weight[0].size // channels
    first_weights = jnp.concatenate(
        [conv_weight[0].reshape(-1, channels), point_weight[:, 0, :]]
    )
    state_pieces, grad_pieces, first_halves = exchanged(
        [
            strided_pieces(sequence_in[0], peers),
            strided_pieces(output_grad[0], peers),
            half_for_each(first_weights, peers, channels),
        ],
        "seq",
    )
    state = state_pieces.reshape(-1, channels)
    second_weights = jnp.concatenate(
        [conv_weight[1].reshape(-1, channels), point_weight[:, 1, :]]
    )
    second_joined = half_for_each(second_weights, peers, channels)
    second_joined, state = lax.optimization_barrier((second_joined, state))
    second_halves = lax.all_to_all(second_joined, "seq", 0, 0, tiled=True)
    wholes = [whole_from_halves(first_halves, "seq"), whole_from_halves(second_halves, "seq")]
    conv_full = [conv_from_pieces(whole[:, :conv_rows], block_shape) for whole in wholes]
    point_blocks = [whole[:, conv_rows:].reshape(-1, channels) for whole in wholes]
    row_reach = (FIRST_DILATION // peers, SECOND_DILATION // peers)
    saved = []
    for block_index in range(2):
        kept_flag = (1 - skip_mask[0, block_index]).astype(jnp.float32)
        normed = state.astype(jnp.float32) * in_gain[block_index] + input_shift_vec[block_index]
        activated = gelu_tanh(normed).astype(jnp.bfloat16)
        earlier, later = row_shifted(activated, row_reach[block_index])
        operands = (
            state,
            earlier,
            activated,
            later,
            conv_full[block_index],
            mid_gain[block_index],
            mid_offset[block_index],
            point_blocks[block_index],
            kept_flag,
        )
        middle, hidden_act, state = forward_local(*operands)
        saved.append((normed, middle, hidden_act, kept_flag))
    gradient = grad_pieces.reshape(-1, channels)
    terms = [None, None]
    for block_index in (1, 0):
        normed, middle, hidden_act, kept_flag = saved[block_index]
        projection = point_blocks[block_index]
        first_operands = (gradient, middle, projection, mid_gain[block_index], kept_flag)
        conv_grad, branch_grad = backward_first(*first_operands)
        terms[block_index] = chip_half(grad_rows(hidden_act, branch_grad), peers, channels)
        earlier, later = row_shifted(conv_grad, row_reach[block_index])
        second_operands = (
            gradient,
            earlier,
            conv_grad,
            later,
            conv_full[block_index],
            normed,
            in_gain[block_index],
        )
        gradient = backward_second(*second_operands)
        if block_index == 1:
            terms[1], gradient = lax.optimization_barrier((terms[1], gradient))
    first_term, second_term, back_pieces = exchanged(
        terms + [gradient.reshape(peers, -1, channels)], "seq"
    )
    own_terms = [chip_sum(piece, peers, channels) for piece in (first_term, second_term)]
    summed = reduced_over_dp(jnp.stack(own_terms, axis=1))
    sample_count = sequence_in.shape[0] * lax.axis_size("dp")
    full_length = sequence_in.shape[1] * peers
    point_grad = summed * (1.0 / math.sqrt(sample_count * full_length))
    input_grad = back_pieces.reshape(sequence_in.shape)
    return (point_grad, input_grad)


def solution(mesh):
    return jax.shard_map(
        shards,
        mesh=mesh,
        in_specs=(
            P("dp", "seq", None),
            P("dp", "seq", None),
            P("dp", None),
            P(),
            P(),
            P(),
            P(),
            P(None, None, "seq", None),
            P("seq", None, None),
        ),
        out_specs=(P("seq", None, None), P("dp", "seq", None)),
        check_vma=False,
    )
```

```python
import math

import jax
import jax.numpy as jnp
from jax import lax
from jax.sharding import PartitionSpec as P

FIRST_DILATION = 1024
SECOND_DILATION = 2048


def passed_along(value, axis, by):
    peers = lax.axis_size(axis)
    pairs = [(i, i + by) for i in range(peers) if 0 <= i + by < peers]
    return lax.ppermute(value, axis, pairs)


def gathered(value, axis):
    peers = lax.axis_size(axis)
    copies = jnp.broadcast_to(value[None], (peers,) + value.shape)
    return lax.all_to_all(copies, axis, 0, 0, tiled=True)


def summed_over(value, axis, sent_as=jnp.float32):
    peers = lax.axis_size(axis)
    pieces = value.reshape((peers, -1) + value.shape[1:]).astype(sent_as)
    arrived = lax.all_to_all(pieces, axis, 0, 0, tiled=True)
    return arrived.astype(jnp.float32).sum(axis=0)


def reduced_over_dp(value):
    dp_size = lax.axis_size("dp")
    own_piece = summed_over(value.reshape(dp_size, -1), "dp", jnp.bfloat16)
    return gathered(own_piece, "dp").reshape(value.shape)


def gelu_tanh(values):
    return jax.nn.gelu(values, approximate=True)


def contract_last(left, right):
    return lax.dot_general(
        left, right, (((1,), (1,)), ((), ())), preferred_element_type=jnp.float32
    )


def neighbours(source, shards_away):
    earlier = passed_along(source, "seq", shards_away)
    later = passed_along(source, "seq", -shards_away)
    return (earlier, later)


def forward_local(
    state, earlier, activated, later, weight, gain_vec, offset_vec, projection, kept_flag
):
    conv_out = jnp.dot(earlier, weight[0], preferred_element_type=jnp.float32)
    conv_out = conv_out + jnp.dot(activated, weight[1], preferred_element_type=jnp.float32)
    conv_out = conv_out + jnp.dot(later, weight[2], preferred_element_type=jnp.float32)
    middle = conv_out * gain_vec + offset_vec
    hidden_act = gelu_tanh(middle).astype(jnp.bfloat16)
    branch = jnp.dot(hidden_act, projection, preferred_element_type=jnp.float32)
    result = (state.astype(jnp.float32) + kept_flag * branch).astype(jnp.bfloat16)
    return (middle, hidden_act, result)


def backward_first(gradient, middle, projection, gain_vec, kept_flag):
    branch_grad = (kept_flag * gradient.astype(jnp.float32)).astype(jnp.bfloat16)
    hidden_grad = contract_last(branch_grad, projection)
    middle_grad = jax.vjp(gelu_tanh, middle)[1](hidden_grad)[0]
    conv_grad = (middle_grad * gain_vec).astype(jnp.bfloat16)
    return (conv_grad, branch_grad)


def backward_second(gradient, earlier, conv_grad, later, weight, normed, gain_vec):
    act_grad = (
        contract_last(later, weight[0])
        + contract_last(conv_grad, weight[1])
        + contract_last(earlier, weight[2])
    )
    normed_grad = jax.vjp(gelu_tanh, normed)[1](act_grad)[0] * gain_vec
    return (gradient.astype(jnp.float32) + normed_grad).astype(jnp.bfloat16)


def grad_rows(hidden_act, branch_grad):
    return lax.dot_general(
        hidden_act, branch_grad, (((0,), (0,)), ((), ())), preferred_element_type=jnp.float32
    )


def exchanged(parts, axis):
    joined = jnp.concatenate(parts, axis=1)
    arrived = lax.all_to_all(joined, axis, 0, 0, tiled=True)
    pieces = []
    offset = 0
    for part in parts:
        pieces.append(arrived[:, offset : offset + part.shape[1]])
        offset += part.shape[1]
    return pieces


def strided_pieces(block, peers):
    return block.reshape(peers, -1, block.shape[-1])


def half_for_each(shard, peers, lanes):
    halves = shard.reshape(2, -1, lanes)
    return jnp.tile(halves, (peers // 2, 1, 1))


def whole_from_halves(own_halves, axis):
    peers = lax.axis_size(axis)
    partner = lax.ppermute(own_halves, axis, [(i, i ^ 1) for i in range(peers)])
    first_core = lax.axis_index(axis) % 2 == 0
    low = jnp.where(first_core, own_halves, partner)
    high = jnp.where(first_core, partner, own_halves)
    return jnp.concatenate([low, high], axis=1)


def conv_from_pieces(pieces, block_shape):
    taps, rows, hidden = block_shape
    parts = pieces.reshape(-1, taps, rows, hidden)
    return jnp.moveaxis(parts, 0, 1).reshape(taps, -1, hidden)


def chip_half(term, peers, channels):
    half = channels // 2
    first_core = lax.axis_index("seq") % 2 == 0
    kept = jnp.where(first_core, term[:, :half], term[:, half:])
    given = jnp.where(first_core, term[:, half:], term[:, :half])
    partner = lax.ppermute(given, "seq", [(i, i ^ 1) for i in range(peers)])
    summed = (kept + partner).astype(jnp.bfloat16)
    return summed.reshape(peers, -1, channels)


def chip_sum(piece, peers, channels):
    half = channels // 2
    parts = piece.reshape(peers // 2, 2, -1, half).astype(jnp.float32).sum(axis=0)
    return jnp.moveaxis(parts, 0, 1).reshape(-1, channels)


def row_shifted(source, rows_away):
    padding = jnp.zeros((rows_away, source.shape[1]), source.dtype)
    earlier = jnp.concatenate([padding, source[: source.shape[0] - rows_away]], axis=0)
    later = jnp.concatenate([source[rows_away:], padding], axis=0)
    return (earlier, later)


def shards(
    sequence_in,
    output_grad,
    skip_mask,
    in_gain,
    input_shift_vec,
    mid_gain,
    mid_offset,
    conv_weight,
    point_weight,
):
    peers = lax.axis_size("seq")
    channels = sequence_in.shape[2]
    block_shape = conv_weight.shape[1:]
    conv_rows = conv_weight[0].size // channels
    first_weights = jnp.concatenate(
        [conv_weight[0].reshape(-1, channels), point_weight[:, 0, :]]
    )
    state_pieces, first_halves = exchanged(
        [
            strided_pieces(sequence_in[0], peers),
            half_for_each(first_weights, peers, channels),
        ],
        "seq",
    )
    state = state_pieces.reshape(-1, channels)
    grad_rows_sent = strided_pieces(output_grad[0], peers)
    second_weights = jnp.concatenate(
        [conv_weight[1].reshape(-1, channels), point_weight[:, 1, :]]
    )
    second_joined = jnp.concatenate(
        [grad_rows_sent, half_for_each(second_weights, peers, channels)], axis=1
    )
    second_joined, state = lax.optimization_barrier((second_joined, state))
    second_arrived = lax.all_to_all(second_joined, "seq", 0, 0, tiled=True)
    grad_pieces = second_arrived[:, : grad_rows_sent.shape[1]]
    second_halves = second_arrived[:, grad_rows_sent.shape[1] :]
    wholes = [whole_from_halves(first_halves, "seq"), whole_from_halves(second_halves, "seq")]
    conv_full = [conv_from_pieces(whole[:, :conv_rows], block_shape) for whole in wholes]
    point_blocks = [whole[:, conv_rows:].reshape(-1, channels) for whole in wholes]
    row_reach = (FIRST_DILATION // peers, SECOND_DILATION // peers)
    saved = []
    for block_index in range(2):
        kept_flag = (1 - skip_mask[0, block_index]).astype(jnp.float32)
        normed = state.astype(jnp.float32) * in_gain[block_index] + input_shift_vec[block_index]
        activated = gelu_tanh(normed).astype(jnp.bfloat16)
        earlier, later = row_shifted(activated, row_reach[block_index])
        operands = (
            state,
            earlier,
            activated,
            later,
            conv_full[block_index],
            mid_gain[block_index],
            mid_offset[block_index],
            point_blocks[block_index],
            kept_flag,
        )
        middle, hidden_act, state = forward_local(*operands)
        saved.append((normed, middle, hidden_act, kept_flag))
    gradient = grad_pieces.reshape(-1, channels)
    terms = [None, None]
    for block_index in (1, 0):
        normed, middle, hidden_act, kept_flag = saved[block_index]
        projection = point_blocks[block_index]
        first_operands = (gradient, middle, projection, mid_gain[block_index], kept_flag)
        conv_grad, branch_grad = backward_first(*first_operands)
        terms[block_index] = chip_half(grad_rows(hidden_act, branch_grad), peers, channels)
        earlier, later = row_shifted(conv_grad, row_reach[block_index])
        second_operands = (
            gradient,
            earlier,
            conv_grad,
            later,
            conv_full[block_index],
            normed,
            in_gain[block_index],
        )
        gradient = backward_second(*second_operands)
        if block_index == 1:
            terms[1], gradient = lax.optimization_barrier((terms[1], gradient))
    first_term, second_term, back_pieces = exchanged(
        terms + [gradient.reshape(peers, -1, channels)], "seq"
    )
    own_terms = [chip_sum(piece, peers, channels) for piece in (first_term, second_term)]
    sample_count = sequence_in.shape[0] * lax.axis_size("dp")
    full_length = sequence_in.shape[1] * peers
    scale = 1.0 / math.sqrt(sample_count * full_length)
    point_grad = reduced_over_dp(jnp.stack(own_terms, axis=1) * scale)
    input_grad = back_pieces.reshape(sequence_in.shape)
    return (point_grad, input_grad)


def solution(mesh):
    return jax.shard_map(
        shards,
        mesh=mesh,
        in_specs=(
            P("dp", "seq", None),
            P("dp", "seq", None),
            P("dp", None),
            P(),
            P(),
            P(),
            P(),
            P(None, None, "seq", None),
            P("seq", None, None),
        ),
        out_specs=(P("seq", None, None), P("dp", "seq", None)),
        check_vma=False,
    )
```

```python
import math

import jax
import jax.numpy as jnp
from jax import lax
from jax.sharding import PartitionSpec as P

FIRST_DILATION = 1024
SECOND_DILATION = 2048


def passed_along(value, axis, by):
    peers = lax.axis_size(axis)
    pairs = [(i, i + by) for i in range(peers) if 0 <= i + by < peers]
    return lax.ppermute(value, axis, pairs)


def gathered(value, axis):
    peers = lax.axis_size(axis)
    copies = jnp.broadcast_to(value[None], (peers,) + value.shape)
    return lax.all_to_all(copies, axis, 0, 0, tiled=True)


def summed_over(value, axis, sent_as=jnp.float32):
    peers = lax.axis_size(axis)
    pieces = value.reshape((peers, -1) + value.shape[1:]).astype(sent_as)
    arrived = lax.all_to_all(pieces, axis, 0, 0, tiled=True)
    return arrived.astype(jnp.float32).sum(axis=0)


def reduced_over_dp(value):
    dp_size = lax.axis_size("dp")
    own_piece = summed_over(value.reshape(dp_size, -1), "dp", jnp.bfloat16)
    return gathered(own_piece, "dp").reshape(value.shape)


def gelu_tanh(values):
    return jax.nn.gelu(values, approximate=True)


def contract_last(left, right):
    return lax.dot_general(
        left, right, (((1,), (1,)), ((), ())), preferred_element_type=jnp.float32
    )


def neighbours(source, shards_away):
    earlier = passed_along(source, "seq", shards_away)
    later = passed_along(source, "seq", -shards_away)
    return (earlier, later)


def forward_local(
    state, earlier, activated, later, weight, gain_vec, offset_vec, projection, kept_flag
):
    conv_out = jnp.dot(earlier, weight[0], preferred_element_type=jnp.float32)
    conv_out = conv_out + jnp.dot(activated, weight[1], preferred_element_type=jnp.float32)
    conv_out = conv_out + jnp.dot(later, weight[2], preferred_element_type=jnp.float32)
    middle = conv_out * gain_vec + offset_vec
    hidden_act = gelu_tanh(middle).astype(jnp.bfloat16)
    branch = jnp.dot(hidden_act, projection, preferred_element_type=jnp.float32)
    result = (state.astype(jnp.float32) + kept_flag * branch).astype(jnp.bfloat16)
    return (middle, hidden_act, result)


def backward_first(gradient, middle, projection, gain_vec, kept_flag):
    branch_grad = (kept_flag * gradient.astype(jnp.float32)).astype(jnp.bfloat16)
    hidden_grad = contract_last(branch_grad, projection)
    middle_grad = jax.vjp(gelu_tanh, middle)[1](hidden_grad)[0]
    conv_grad = (middle_grad * gain_vec).astype(jnp.bfloat16)
    return (conv_grad, branch_grad)


def backward_second(gradient, earlier, conv_grad, later, weight, normed, gain_vec):
    act_grad = (
        contract_last(later, weight[0])
        + contract_last(conv_grad, weight[1])
        + contract_last(earlier, weight[2])
    )
    normed_grad = jax.vjp(gelu_tanh, normed)[1](act_grad)[0] * gain_vec
    return (gradient.astype(jnp.float32) + normed_grad).astype(jnp.bfloat16)


def grad_rows(hidden_act, branch_grad):
    return lax.dot_general(
        hidden_act, branch_grad, (((0,), (0,)), ((), ())), preferred_element_type=jnp.float32
    )


def exchanged(parts, axis):
    joined = jnp.concatenate(parts, axis=1)
    arrived = lax.all_to_all(joined, axis, 0, 0, tiled=True)
    pieces = []
    offset = 0
    for part in parts:
        pieces.append(arrived[:, offset : offset + part.shape[1]])
        offset += part.shape[1]
    return pieces


def strided_pieces(block, peers):
    return block.reshape(peers, -1, block.shape[-1])


def half_for_each(shard, peers, lanes):
    halves = shard.reshape(2, -1, lanes)
    return jnp.tile(halves, (peers // 2, 1, 1))


def whole_from_halves(own_halves, axis):
    peers = lax.axis_size(axis)
    partner = lax.ppermute(own_halves, axis, [(i, i ^ 1) for i in range(peers)])
    first_core = lax.axis_index(axis) % 2 == 0
    low = jnp.where(first_core, own_halves, partner)
    high = jnp.where(first_core, partner, own_halves)
    return jnp.concatenate([low, high], axis=1)


def conv_from_pieces(pieces, block_shape):
    taps, rows, hidden = block_shape
    parts = pieces.reshape(-1, taps, rows, hidden)
    return jnp.moveaxis(parts, 0, 1).reshape(taps, -1, hidden)


def chip_half(term, peers, channels):
    half = channels // 2
    first_core = lax.axis_index("seq") % 2 == 0
    kept = jnp.where(first_core, term[:, :half], term[:, half:])
    given = jnp.where(first_core, term[:, half:], term[:, :half])
    partner = lax.ppermute(given, "seq", [(i, i ^ 1) for i in range(peers)])
    summed = (kept + partner).astype(jnp.bfloat16)
    return summed.reshape(peers, -1, channels)


def chip_sum(piece, peers, channels):
    half = channels // 2
    parts = piece.reshape(peers // 2, 2, -1, half).astype(jnp.float32).sum(axis=0)
    return jnp.moveaxis(parts, 0, 1).reshape(-1, channels)


def row_shifted(source, rows_away):
    padding = jnp.zeros((rows_away, source.shape[1]), source.dtype)
    earlier = jnp.concatenate([padding, source[: source.shape[0] - rows_away]], axis=0)
    later = jnp.concatenate([source[rows_away:], padding], axis=0)
    return (earlier, later)


def shards(
    sequence_in,
    output_grad,
    skip_mask,
    in_gain,
    input_shift_vec,
    mid_gain,
    mid_offset,
    conv_weight,
    point_weight,
):
    peers = lax.axis_size("seq")
    channels = sequence_in.shape[2]
    block_shape = conv_weight.shape[1:]
    conv_rows = conv_weight[0].size // channels
    first_weights = jnp.concatenate(
        [conv_weight[0].reshape(-1, channels), point_weight[:, 0, :]]
    )
    state_sent = strided_pieces(sequence_in[0], peers)
    first_joined = jnp.concatenate(
        [state_sent, half_for_each(first_weights, peers, channels)], axis=1
    )
    grad_rows_sent = strided_pieces(output_grad[0], peers)
    second_weights = jnp.concatenate(
        [conv_weight[1].reshape(-1, channels), point_weight[:, 1, :]]
    )
    second_joined = jnp.concatenate(
        [grad_rows_sent, half_for_each(second_weights, peers, channels)], axis=1
    )
    first_joined, second_joined = lax.optimization_barrier((first_joined, second_joined))
    first_arrived = lax.all_to_all(first_joined, "seq", 0, 0, tiled=True)
    state = first_arrived[:, : state_sent.shape[1]].reshape(-1, channels)
    first_halves = first_arrived[:, state_sent.shape[1] :]
    second_joined, state = lax.optimization_barrier((second_joined, state))
    second_arrived = lax.all_to_all(second_joined, "seq", 0, 0, tiled=True)
    grad_pieces = second_arrived[:, : grad_rows_sent.shape[1]]
    second_halves = second_arrived[:, grad_rows_sent.shape[1] :]
    wholes = [whole_from_halves(first_halves, "seq"), whole_from_halves(second_halves, "seq")]
    conv_full = [conv_from_pieces(whole[:, :conv_rows], block_shape) for whole in wholes]
    point_blocks = [whole[:, conv_rows:].reshape(-1, channels) for whole in wholes]
    row_reach = (FIRST_DILATION // peers, SECOND_DILATION // peers)
    saved = []
    for block_index in range(2):
        kept_flag = (1 - skip_mask[0, block_index]).astype(jnp.float32)
        normed = state.astype(jnp.float32) * in_gain[block_index] + input_shift_vec[block_index]
        activated = gelu_tanh(normed).astype(jnp.bfloat16)
        earlier, later = row_shifted(activated, row_reach[block_index])
        operands = (
            state,
            earlier,
            activated,
            later,
            conv_full[block_index],
            mid_gain[block_index],
            mid_offset[block_index],
            point_blocks[block_index],
            kept_flag,
        )
        middle, hidden_act, state = forward_local(*operands)
        saved.append((normed, middle, hidden_act, kept_flag))
    gradient = grad_pieces.reshape(-1, channels)
    terms = [None, None]
    for block_index in (1, 0):
        normed, middle, hidden_act, kept_flag = saved[block_index]
        projection = point_blocks[block_index]
        first_operands = (gradient, middle, projection, mid_gain[block_index], kept_flag)
        conv_grad, branch_grad = backward_first(*first_operands)
        terms[block_index] = chip_half(grad_rows(hidden_act, branch_grad), peers, channels)
        earlier, later = row_shifted(conv_grad, row_reach[block_index])
        second_operands = (
            gradient,
            earlier,
            conv_grad,
            later,
            conv_full[block_index],
            normed,
            in_gain[block_index],
        )
        gradient = backward_second(*second_operands)
        if block_index == 1:
            terms[1], gradient = lax.optimization_barrier((terms[1], gradient))
    first_term, second_term, back_pieces = exchanged(
        terms + [gradient.reshape(peers, -1, channels)], "seq"
    )
    own_terms = [chip_sum(piece, peers, channels) for piece in (first_term, second_term)]
    sample_count = sequence_in.shape[0] * lax.axis_size("dp")
    full_length = sequence_in.shape[1] * peers
    scale = 1.0 / math.sqrt(sample_count * full_length)
    point_grad = reduced_over_dp(jnp.stack(own_terms, axis=1) * scale)
    input_grad = back_pieces.reshape(sequence_in.shape)
    return (point_grad, input_grad)


def solution(mesh):
    return jax.shard_map(
        shards,
        mesh=mesh,
        in_specs=(
            P("dp", "seq", None),
            P("dp", "seq", None),
            P("dp", None),
            P(),
            P(),
            P(),
            P(),
            P(None, None, "seq", None),
            P("seq", None, None),
        ),
        out_specs=(P("seq", None, None), P("dp", "seq", None)),
        check_vma=False,
    )
```
